32 devices in a mesh: group: 2 (over x), tile: 16 (over z, y, core).
Axes of the slice: x: 2, y: 2, z: 4, core: 2. Of those that a mesh axis runs over, the one named last changes fastest.
Arguments:
- object_field: float32 [4, 2, 2048, 2048], P('group', None, 'tile'), parts along dimension 0, may hold values from -6 to 6
- probe: float32 [2, 256, 256], replicated, may hold values from -6 to 6
- measured: bfloat16 [64, 256, 256], P(('group', 'tile')), parts along dimension 0, may hold values from 0.099609375 to 3
- frame_table: int32 [64, 3], P(('group', 'tile')), parts along dimension 0, may hold values from 0 to 1792, as said below
- frame_count: int32 [32], P(('group', 'tile')), parts along dimension 0, may hold values from 0 to 2, as said below
Outputs:
- updated_object: float32 [4, 2, 2048, 2048], P('group', None, 'tile'), parts along dimension 0
- phase_map: float32 [4, 2048, 2048], P('group', 'tile'), parts along dimension 0
The draws below stay inside these ranges and needn't reach their ends.
There are 2 independent parts, one for each index of `group`. The reference program is written for one: setup_inputs(seed, part) draws one part's arguments, and reference() takes and returns one part's arrays. A program takes and returns all parts, laid end to end along the dimension named above; an argument that names none is the same for every part. Nothing has to cross between parts.
Inputs may be any that keep to these rules, and one draw needn't show every extreme that they name: `frame_table`: per slot: the row offset is below 128, and the frame's rows d * 128 + offset to that plus 256 - 1 and columns lie inside the projection; the angle is below 2. Only the first frame_count[d] slots of device d are live. `frame_count`: exactly 2 on some device in every draw; zero on every device d with d * 128 > 1792.
All inputs are finite; a program needn't handle non-finite values.
Results may differ from the reference program's by a relative error of at most 0.0009.
Values may be sent and summed in bfloat16 or wider, within the bound.
A program may use at most 192 MiB of HBM per device.

```python
import math
import jax
import jax.numpy as jnp
from jax import lax

NP = 2048
FRAME = 256
ANGLES = 2
CAP = 2
SLOTS = 32
N_TILE = 16


def frame_layout(key):
    strip_rows = NP // N_TILE
    devices = jnp.arange(N_TILE, dtype=jnp.int32)
    spare_rows = jnp.clip(NP - FRAME - devices * strip_rows + 1, 0, strip_rows)
    subkeys = jax.random.split(jax.random.fold_in(key, 7), 6)
    first_draw = jax.random.randint(subkeys[0], (N_TILE,), 0, CAP, dtype=jnp.int32)
    second_draw = jax.random.randint(subkeys[1], (N_TILE,), 0, CAP, dtype=jnp.int32)
    counts = 1 + first_draw * second_draw // CAP
    busiest = jax.random.randint(subkeys[2], (), 0, N_TILE - FRAME // strip_rows + 1, dtype=jnp.int32)
    counts = jnp.where(devices == busiest, CAP, counts)
    counts = jnp.where(spare_rows > 0, counts, 0)
    offsets = jax.random.randint(subkeys[3], (N_TILE, CAP), 0, strip_rows, dtype=jnp.int32) % jnp.maximum(spare_rows, 1)[:, None]
    columns = jax.random.randint(subkeys[4], (N_TILE, CAP), 0, NP - FRAME + 1, dtype=jnp.int32)
    angle_ids = jax.random.randint(subkeys[5], (N_TILE, CAP), 0, ANGLES, dtype=jnp.int32)
    slot_table = jnp.stack([offsets, columns, angle_ids], -1).reshape(N_TILE * CAP, 3)
    return (slot_table.astype(jnp.int32), counts.astype(jnp.int32))


def draw_frame_table(key, part):
    return frame_layout(key)[0]


def draw_frame_count(key, part):
    return frame_layout(key)[1]


def block_levels(stream_key, dims, cuts, smallest, top_value):
    factor_of = 1.0
    for dim, parts in cuts:
        draws = jax.random.uniform(jax.random.fold_in(jax.random.fold_in(stream_key, 6), dim), (parts,), jnp.float32, smallest / len(cuts), top_value / len(cuts))
        factor_of = factor_of * jnp.repeat(jnp.exp(draws), dims[dim] // parts).reshape((-1,) + (1,) * (len(dims) - 1 - dim))
    return factor_of


def normal_values(own_key, shape, spread, most, pieces=(), kind=jnp.bfloat16):
    factor_of = block_levels(own_key, shape, pieces, -0.22, 0.18) if pieces else 1.0
    array = jax.random.normal(own_key, shape, jnp.float32) * spread * factor_of
    return jnp.minimum(jnp.maximum(array, -most), most).astype(kind)


def setup_inputs(seed: int = 0, part: int = 0) -> dict:
    arg_keys = jax.random.split(jax.random.key(seed), 6)
    part_splits = jax.random.split(jax.random.fold_in(arg_keys[5], part), 6)
    return {
        "object_field": normal_values(part_splits[0], (ANGLES, 2, NP, NP), 1.0, 6.0, ((2, 16),), jnp.float32),
        "probe": normal_values(arg_keys[1], (2, FRAME, FRAME), 1.0, 6.0, (), jnp.float32),
        "measured": jnp.clip(jnp.exp(math.log(3.0) - 3.4051113 * jax.random.uniform(part_splits[2], (SLOTS, FRAME, FRAME), jnp.float32) ** block_levels(part_splits[2], (SLOTS, FRAME, FRAME), ((0, 16),), -0.2, 0.2)), 0.099609375, 3.0).astype(jnp.bfloat16),
        "frame_table": draw_frame_table(jax.random.fold_in(jax.random.fold_in(arg_keys[5], part), 71), part),
        "frame_count": draw_frame_count(jax.random.fold_in(jax.random.fold_in(arg_keys[5], part), 71), part),
    }


magnitude_floor = 0.5
soften_term = 0.5
screen_term = 0.0001
epsilon_term = 1e-06

def fourier_tables(frame_side):
    indices = jnp.arange(frame_side, dtype=jnp.int32)
    products = indices[:, None] * indices[None, :] % frame_side
    phases = products.astype(jnp.float32) * (-2.0 * math.pi / frame_side)
    norm_scale = 1.0 / math.sqrt(frame_side)
    return ((jnp.cos(phases) * norm_scale).astype(jnp.bfloat16), (jnp.sin(phases) * norm_scale).astype(jnp.bfloat16))

def complex_left(table_re, table_im, operand):
    side = table_re.shape[0]
    stacked = jnp.concatenate([table_re, table_im], 0)
    joined = jnp.concatenate([operand[0], operand[1]], 1)
    products = jnp.dot(stacked, joined, preferred_element_type=jnp.float32)
    return jnp.stack([products[:side, :side] - products[side:, side:], products[:side, side:] + products[side:, :side]])

def complex_right(operand, table_re, table_im):
    side = table_re.shape[0]
    stacked = jnp.concatenate([operand[0], operand[1]], 0)
    joined = jnp.concatenate([table_re, table_im], 1)
    products = jnp.dot(stacked, joined, preferred_element_type=jnp.float32)
    return jnp.stack([products[:side, :side] - products[side:, side:], products[:side, side:] + products[side:, :side]])

def correct_frame(exit_field, magnitude, fourier):
    cos_part, sin_part = fourier
    half_spectrum = complex_left(cos_part, sin_part, exit_field).astype(jnp.bfloat16)
    spectrum = complex_right(half_spectrum, cos_part, sin_part)
    amplitude = jnp.sqrt(spectrum[0] * spectrum[0] + spectrum[1] * spectrum[1])
    factor = magnitude.astype(spectrum.dtype) / jnp.maximum(amplitude, magnitude_floor) - 1.0
    change = (spectrum * factor[None]).astype(jnp.bfloat16)
    half_back = complex_left(cos_part, -sin_part, change).astype(jnp.bfloat16)
    return complex_right(half_back, cos_part, -sin_part)

def exit_wave(probe, patch):
    object_part = patch.astype(probe.dtype)
    real_part = probe[0] * object_part[0] - probe[1] * object_part[1]
    imag_part = probe[0] * object_part[1] + probe[1] * object_part[0]
    return jnp.stack([real_part, imag_part]).astype(jnp.bfloat16)

def object_step(probe, correction, probe_peak):
    real_part = (probe[0] * correction[0] + probe[1] * correction[1]) / probe_peak
    imag_part = (probe[0] * correction[1] - probe[1] * correction[0]) / probe_peak
    return jnp.stack([real_part, imag_part])

def phase_bond(first_cell, second_cell):
    cross_term = first_cell[:, 0] * second_cell[:, 1] - first_cell[:, 1] * second_cell[:, 0]
    power_sum = first_cell[:, 0] ** 2 + first_cell[:, 1] ** 2 + second_cell[:, 0] ** 2 + second_cell[:, 1] ** 2 + soften_term
    return 2.0 * cross_term / power_sum

def cosine_last(values):
    length = values.shape[-1]
    mirrored = jnp.concatenate([values, jnp.flip(values, -1)], -1)
    spectrum = jnp.fft.fft(mirrored, axis=-1)[..., :length]
    freqs = jnp.arange(length, dtype=jnp.int32).astype(values.dtype)
    twisted = jnp.real(spectrum * jnp.exp(-1j * math.pi * freqs / (2 * length)))
    norm_scale = jnp.where(freqs == 0, math.sqrt(1.0 / length), math.sqrt(2.0 / length)) * 0.5
    return (twisted * norm_scale).astype(values.dtype)

def inverse_last(coeffs):
    length = coeffs.shape[-1]
    freqs = jnp.arange(length, dtype=jnp.int32).astype(coeffs.dtype)
    norm_scale = jnp.where(freqs == 0, math.sqrt(1.0 / length), math.sqrt(2.0 / length))
    weighted = coeffs * norm_scale * jnp.exp(1j * math.pi * freqs / (2 * length))
    padded = jnp.concatenate([weighted, jnp.zeros_like(weighted)], -1)
    values = jnp.real(jnp.fft.ifft(padded, axis=-1)[..., :length]) * (2 * length)
    return values.astype(coeffs.dtype)

def reference(object_field, probe, measured, frame_table, frame_count):
    window_object = object_field.astype(jnp.bfloat16)
    fourier = fourier_tables(FRAME)
    probe_peak = jnp.max(probe[0] * probe[0] + probe[1] * probe[1]) + epsilon_term
    strip_rows = NP // N_TILE
    anchor = jnp.zeros((), jnp.int32)

    def visit(slot_index, deposits):
        slot_index = jnp.asarray(slot_index).astype(jnp.int32)
        owner = slot_index // CAP
        live = slot_index % CAP < frame_count[owner]

        def apply(current_sum):
            record = frame_table[slot_index]
            corner = (record[2].astype(jnp.int32), anchor, (owner * strip_rows + record[0]).astype(jnp.int32), record[1].astype(jnp.int32))
            patch = lax.dynamic_slice(window_object, corner, (1, 2, FRAME, FRAME))[0]
            correction = correct_frame(exit_wave(probe, patch), measured[slot_index], fourier)
            update = object_step(probe, correction, probe_peak)
            current = lax.dynamic_slice(current_sum, corner, (1, 2, FRAME, FRAME))
            return lax.dynamic_update_slice(current_sum, current + update[None], corner)
        return lax.cond(live, apply, lambda current_sum: current_sum, deposits)
    deposits = lax.fori_loop(0, SLOTS, visit, jnp.zeros(object_field.shape, object_field.dtype))
    updated_object = object_field + deposits
    padded = jnp.pad(updated_object, ((0, 0), (0, 0), (1, 1), (1, 1)))
    row_grad = phase_bond(padded[:, :, :-1, 1:-1], padded[:, :, 1:, 1:-1])
    col_grad = phase_bond(padded[:, :, 1:-1, :-1], padded[:, :, 1:-1, 1:])
    source = -(row_grad[:, 1:] - row_grad[:, :-1] + col_grad[:, :, 1:] - col_grad[:, :, :-1])
    along_rows = jnp.swapaxes(cosine_last(jnp.swapaxes(source, 1, 2)), 1, 2)
    both_dims = cosine_last(along_rows)
    freqs = jnp.arange(NP, dtype=jnp.int32).astype(source.dtype)
    eigen = 2.0 - 2.0 * jnp.cos(freqs * (math.pi / NP))
    coefficients = both_dims / (screen_term + eigen[None, :, None] + eigen[None, None, :])
    back_rows = jnp.swapaxes(inverse_last(jnp.swapaxes(coefficients, 1, 2)), 1, 2)
    phase_map = inverse_last(back_rows)
    return (updated_object, phase_map)
```

```python
import functools
import math

import numpy as np
import jax
import jax.numpy as jnp
from jax import lax
from jax.experimental import pallas as pl
from jax.experimental.pallas import tpu as pltpu
from jax.sharding import PartitionSpec as P

magnitude_floor = 0.5
soften_term = 0.5
screen_term = 0.0001
epsilon_term = 1e-06
f32 = jnp.float32
bf16 = jnp.bfloat16
LANES = 128
GROUP = 8
TILE = 256
VMEM_BYTES = 60 * 1024 * 1024
vmem = pl.BlockSpec(memory_space=pltpu.VMEM)
smem = pl.BlockSpec(memory_space=pltpu.SMEM)
hbm = pl.BlockSpec(memory_space=pl.ANY)


def passed_along(x, axis, by):
    size = lax.axis_size(axis)
    pairs = [(i, i + by) for i in range(size) if 0 <= i + by < size]
    return lax.ppermute(x, axis, pairs)


def params(**more):
    return pltpu.CompilerParams(vmem_limit_bytes=VMEM_BYTES, **more)


def fourier_tables(side):
    indices = np.arange(side)
    products = indices[:, None] * indices[None, :] % side
    phases = products.astype(np.float64) * (-2.0 * math.pi / side)
    scale = 1.0 / math.sqrt(side)
    return (
        jnp.asarray(np.cos(phases) * scale, f32).astype(bf16),
        jnp.asarray(np.sin(phases) * scale, f32).astype(bf16),
    )


def cosine_factors(grid_side):
    half = grid_side // 2
    step = 32
    out = []
    for odd in (0, 1):
        freqs = 2 * np.arange(half) + odd
        scale = np.where(freqs == 0, math.sqrt(1.0 / grid_side), math.sqrt(2.0 / grid_side))
        coarse = (2 * step * np.arange(half // step)[:, None] * freqs[None, :]) % (4 * grid_side)
        fine = ((2 * np.arange(step)[:, None] + 1) * freqs[None, :]) % (4 * grid_side)
        unit = math.pi / (2 * grid_side)
        out.append(
            np.stack(
                [
                    np.cos(coarse * unit) * scale,
                    np.sin(coarse * unit) * scale,
                    np.cos(fine * unit),
                    np.sin(fine * unit),
                ]
            )
        )
    return jnp.asarray(np.stack(out), f32)


def decay_tables(grid_side, strip_rows):
    half = grid_side // 2
    freqs = np.concatenate([2 * np.arange(half), 2 * np.arange(half) + 1]).astype(np.float64)
    shift = screen_term + 2.0 - 2.0 * np.cos(freqs * math.pi / grid_side)
    rate = 2.0 * np.arcsinh(np.sqrt(shift) / 2.0)
    gain = 1.0 / (2.0 * np.sinh(rate))
    rows = np.arange(GROUP)[:, None]
    down = [np.where(rows >= s, np.exp(-s * rate), 0.0) for s in (1, 2, 4)]
    up = [np.where(rows < GROUP - s, np.exp(-s * rate), 0.0) for s in (1, 2, 4)]
    down.append(np.exp(-(rows + 1) * rate))
    up.append(np.exp(-(GROUP - rows) * rate))
    local = np.stack(down + up)
    strips = grid_side // strip_rows
    powers = np.exp(-strip_rows * np.arange(strips + 1)[:, None] * rate)
    extra = np.stack(
        [gain, 1.0 / (1.0 - np.exp(-2.0 * grid_side * rate)), np.exp(-GROUP * rate)]
        + [rate * 0.0] * 5
    )
    return jnp.asarray(local, f32), jnp.asarray(powers, f32), jnp.asarray(extra, f32)


def table_kernel(factors, even_hi, even_lo, odd_hi, odd_lo):
    step = factors.shape[2]
    blocks = even_hi.shape[0] // step
    for part, (high, low) in enumerate(((even_hi, even_lo), (odd_hi, odd_lo))):
        fine_cos = factors[part, 2]
        fine_sin = factors[part, 3]
        for block in range(blocks):
            value = (
                factors[part, 0, block : block + 1] * fine_cos
                - factors[part, 1, block : block + 1] * fine_sin
            )
            rounded = value.astype(bf16)
            high[block * step : (block + 1) * step] = rounded
            low[block * step : (block + 1) * step] = (value - rounded.astype(f32)).astype(bf16)


def window_start(column, width, span):
    return jnp.minimum(column // LANES, (width - span) // LANES) * LANES


def cut_kernel(tables, field, out, buffer, sems):
    count, cap = tables.shape[0], tables.shape[1]
    width = field.shape[3]
    side = out.shape[-1]
    span = side + LANES
    jobs = [(j, s) for j in range(count) for s in range(cap)]

    def fetch(index):
        j, s = jobs[index]
        start = pl.multiple_of(window_start(tables[j, s, 1], width, span), LANES)
        return pltpu.make_async_copy(
            field.at[tables[j, s, 2], :, :, pl.ds(start, span)], buffer.at[index], sems.at[index]
        )

    for index in range(len(jobs)):
        fetch(index).start()
    for index, (j, s) in enumerate(jobs):
        fetch(index).wait()
        column = tables[j, s, 1]
        shift = column - window_start(column, width, span)
        for part in range(2):
            turned = pltpu.roll(buffer[index, part], lax.rem(span - shift, span), 1)
            out[j, s, part] = turned[:, :side].astype(bf16)


def frame_kernel(table, counts, probe, measured, cos_ref, sin_ref, *refs):
    pieces = refs[: len(refs) - 3]
    own_out, away_out, window = refs[len(refs) - 3 :]
    cap, side = measured.shape[0], measured.shape[1]
    strip = pieces[0].shape[2]
    reach = len(pieces) - 1
    total = (reach + 1) * strip
    cos_part, sin_part = cos_ref[...], sin_ref[...]
    stacked = jnp.concatenate([cos_part, sin_part], 0)
    joined = jnp.concatenate([cos_part, sin_part], 1)
    probe_re, probe_im = probe[0], probe[1]
    peak = jnp.max(probe_re * probe_re + probe_im * probe_im) + epsilon_term

    def left(re, im, sign):
        products = jnp.dot(
            stacked, jnp.concatenate([re, im], 1), preferred_element_type=f32
        )
        cc, ci = products[:side, :side], products[:side, side:]
        sc, si = products[side:, :side], products[side:, side:]
        return (cc - si, ci + sc) if sign > 0 else (cc + si, ci - sc)

    def right(re, im, sign):
        products = jnp.dot(
            jnp.concatenate([re, im], 0), joined, preferred_element_type=f32
        )
        rc, rs = products[:side, :side], products[:side, side:]
        ic, js = products[side:, :side], products[side:, side:]
        return (rc - js, rs + ic) if sign > 0 else (rc + js, ic - rs)

    for s in range(cap):
        offset = table[s, 0]
        patch = []
        for part in range(2):
            for j in range(reach + 1):
                window[j * strip : (j + 1) * strip] = pieces[j][s, part].astype(f32)
            turned = pltpu.roll(window[...], lax.rem(total - offset, total), 0)
            patch.append(turned[:side])
        wave_re = (probe_re * patch[0] - probe_im * patch[1]).astype(bf16)
        wave_im = (probe_re * patch[1] + probe_im * patch[0]).astype(bf16)
        half_re, half_im = left(wave_re, wave_im, 1)
        spec_re, spec_im = right(half_re.astype(bf16), half_im.astype(bf16), 1)
        amplitude = jnp.sqrt(spec_re * spec_re + spec_im * spec_im)
        factor = measured[s].astype(f32) / jnp.maximum(amplitude, magnitude_floor) - 1.0
        back_re, back_im = left(
            (spec_re * factor).astype(bf16), (spec_im * factor).astype(bf16), -1
        )
        corr_re, corr_im = right(back_re.astype(bf16), back_im.astype(bf16), -1)
        live = s < counts[0]
        updates = (
            (probe_re * corr_re + probe_im * corr_im) / peak,
            (probe_re * corr_im - probe_im * corr_re) / peak,
        )
        for part in range(2):
            window[...] = jnp.zeros_like(window)
            window[:side] = jnp.where(live, updates[part], 0.0)
            turned = pltpu.roll(window[...], offset, 0)
            own_out[s, part] = turned[:strip]
            for j in range(1, reach + 1):
                away_out[j - 1, s, part] = turned[j * strip : (j + 1) * strip].astype(bf16)


def place_kernel(tables, field, own, *refs):
    away, out = refs[:-1], refs[-1]
    width = field.shape[3]
    cap, side = own.shape[0], own.shape[3]
    span = side + LANES
    out[...] = field[...]
    pad = jnp.zeros((own.shape[2], LANES), f32)
    for j, source in enumerate((own, *away)):
        for s in range(cap):
            column = tables[j, s, 1]
            start = pl.multiple_of(window_start(column, width, span), LANES)
            shift = column - start
            angle = tables[j, s, 2]
            for part in range(2):
                value = jnp.concatenate([source[s, part].astype(f32), pad], 1)
                turned = pltpu.roll(value, shift, 1)
                out[angle, part, :, pl.ds(start, span)] = (
                    out[angle, part, :, pl.ds(start, span)] + turned
                )


def mirror(value):
    side = value.shape[1]
    rows = lax.broadcasted_iota(jnp.int32, (side, side), 0)
    columns = lax.broadcasted_iota(jnp.int32, (side, side), 1)
    swap = jnp.where(rows + columns == side - 1, 1.0, 0.0).astype(bf16)
    total = None
    for _ in range(3):
        piece = value.astype(bf16)
        value = value - piece.astype(f32)
        term = jnp.dot(piece, swap, preferred_element_type=f32)
        total = term if total is None else total + term
    return total


def split_store(value, high, low, columns):
    rounded = value.astype(bf16)
    high[:, columns] = rounded
    low[:, columns] = (value - rounded.astype(f32)).astype(bf16)


def bond(a_re, a_im, b_re, b_im):
    cross = a_re * b_im - a_im * b_re
    power = a_re * a_re + a_im * a_im + b_re * b_re + b_im * b_im + soften_term
    return 2.0 * cross / power


def forward_kernel(
    field, above, below, even_hi, even_lo, odd_hi, odd_lo, local, extra,
    out, ends, source, xeh, xel, xoh, xol,
):
    angles, _, strip, width = field.shape
    half = width // 2
    block = GROUP * 2
    columns = lax.broadcasted_iota(jnp.int32, (block, width), 1)
    for angle in range(angles):
        for first in range(0, strip, block):
            here, up, down, left = [], [], [], []
            for part in range(2):
                body = field[angle, part, first : first + block]
                before = (
                    above[angle, part]
                    if first == 0
                    else field[angle, part, first - 1 : first]
                )
                after = (
                    below[angle, part]
                    if first + block == strip
                    else field[angle, part, first + block : first + block + 1]
                )
                here.append(body)
                up.append(jnp.concatenate([before, body[:-1]], 0))
                down.append(jnp.concatenate([body[1:], after], 0))
                left.append(jnp.where(columns == 0, 0.0, pltpu.roll(body, 1, 1)))
            row_up = bond(*up, *here)
            row_down = bond(*here, *down)
            col_left = bond(*left, *here)
            col_right = jnp.where(
                columns == width - 1, 0.0, pltpu.roll(col_left, width - 1, 1)
            )
            source[angle * strip + first : angle * strip + first + block] = -(
                row_down - row_up + col_right - col_left
            )
    for first in range(0, half, TILE):
        near = source[:, first : first + TILE]
        far = mirror(source[:, width - first - TILE : width - first])
        where = slice(first, first + TILE)
        split_store(near + far, xeh, xel, where)
        split_store(near - far, xoh, xol, where)
    for base, high, low, table_hi, table_lo in (
        (0, xeh, xel, even_hi, even_lo),
        (half, xoh, xol, odd_hi, odd_lo),
    ):
        for first in range(0, half, TILE):
            where = slice(first, first + TILE)
            source[:, base + first : base + first + TILE] = (
                jnp.dot(high[...], table_hi[:, where], preferred_element_type=f32)
                + jnp.dot(low[...], table_hi[:, where], preferred_element_type=f32)
                + jnp.dot(high[...], table_lo[:, where], preferred_element_type=f32)
            )
    groups = strip // GROUP
    for first in range(0, width, LANES):
        where = slice(first, first + LANES)
        gain = extra[0:1, where]
        for angle in range(angles):
            value = source[angle * strip : (angle + 1) * strip, where]
            value = value.reshape(groups, GROUP, LANES)
            fall, rise = value, value
            for index, by in enumerate((1, 2, 4)):
                fall = fall + local[index, :, where][None] * pltpu.roll(fall, by, 1)
                rise = rise + local[4 + index, :, where][None] * pltpu.roll(rise, GROUP - by, 1)
            falls, carry = [], None
            for group in range(groups):
                item = fall[group]
                if carry is not None:
                    item = item + local[3, :, where] * carry
                carry = item[GROUP - 1 :]
                falls.append(item)
            ends[0, angle : angle + 1, where] = carry
            rises, carry = [None] * groups, None
            for group in reversed(range(groups)):
                item = rise[group]
                if carry is not None:
                    item = item + local[7, :, where] * carry
                carry = item[:1]
                rises[group] = item
            ends[1, angle : angle + 1, where] = carry
            for group in range(groups):
                out[angle, group * GROUP : (group + 1) * GROUP, where] = gain * (
                    falls[group] + rises[group] - value[group]
                )


def inverse_kernel(
    place, value, ends, even_hi, even_lo, odd_hi, odd_lo, local, powers, extra,
    out, incoming, xh, xl,
):
    angles, strip, width = value.shape
    half = width // 2
    strips = ends.shape[0]
    me = place[0]
    wall = jnp.zeros((angles, width), f32)
    floor = jnp.zeros((angles, width), f32)
    enter = jnp.zeros((angles, width), f32)
    leave = jnp.zeros((angles, width), f32)
    for b in range(strips):
        right_end, left_end = ends[b, 0], ends[b, 1]
        wall = wall + powers[b : b + 1] * left_end
        floor = floor + powers[strips - 1 - b : strips - b] * right_end
        weight = powers[pl.ds(jnp.maximum(me - 1 - b, 0), 1)]
        enter = enter + jnp.where(b < me, weight, 0.0) * right_end
        weight = powers[pl.ds(jnp.maximum(b - me - 1, 0), 1)]
        leave = leave + jnp.where(b > me, weight, 0.0) * left_end
    whole = powers[strips : strips + 1]
    closing = extra[1:2]
    gain = extra[0:1]
    enter = enter + powers[pl.ds(me, 1)] * (wall + whole * floor) * closing
    leave = leave + powers[pl.ds(strips - 1 - me, 1)] * (floor + whole * wall) * closing
    incoming[0] = enter * gain
    incoming[1] = leave * gain
    groups = strip // GROUP
    for first in range(0, width, LANES):
        where = slice(first, first + LANES)
        for angle in range(angles):
            fall = incoming[0, angle : angle + 1, where]
            rise = incoming[1, angle : angle + 1, where]
            step = extra[2:3, where]
            falls, rises = [], []
            for group in range(groups):
                falls.append(fall)
                rises.append(rise)
                fall = fall * step
                rise = rise * step
            for pair in range(0, groups, 2):
                rows = []
                for group in (pair, pair + 1):
                    rows.append(
                        value[angle, group * GROUP : (group + 1) * GROUP, where]
                        + local[3, :, where] * falls[group]
                        + local[7, :, where] * rises[groups - 1 - group]
                    )
                item = jnp.concatenate(rows, 0)
                rounded = item.astype(bf16)
                start = angle * strip + pair * GROUP
                xh[start : start + 2 * GROUP, where] = rounded
                xl[start : start + 2 * GROUP, where] = (item - rounded.astype(f32)).astype(bf16)
    last = (((1,), (1,)), ((), ()))
    for first in range(0, half, TILE):
        where = slice(first, first + TILE)
        parts = []
        for base, table_hi, table_lo in ((0, even_hi, even_lo), (half, odd_hi, odd_lo)):
            high = xh[:, base : base + half]
            low = xl[:, base : base + half]
            parts.append(
                lax.dot_general(high, table_hi[where], last, preferred_element_type=f32)
                + lax.dot_general(low, table_hi[where], last, preferred_element_type=f32)
                + lax.dot_general(high, table_lo[where], last, preferred_element_type=f32)
            )
        near = parts[0] + parts[1]
        far = mirror(parts[0] - parts[1])
        for angle in range(angles):
            rows = slice(angle * strip, (angle + 1) * strip)
            out[angle, :, where] = near[rows]
            out[angle, :, width - first - TILE : width - first] = far[rows]


def body(object_field, probe, measured, frame_table, frame_count):
    angles, _, strip, width = object_field.shape
    side = probe.shape[1]
    cap = measured.shape[0]
    half = width // 2
    reach = side // strip
    rows = angles * strip
    shape = jax.ShapeDtypeStruct

    above_tables = [frame_table] + [
        passed_along(frame_table, "tile", j) for j in range(1, reach + 1)
    ]
    tables = jnp.stack(above_tables)
    cuts = pl.pallas_call(
        cut_kernel,
        out_shape=shape((reach + 1, cap, 2, strip, side), bf16),
        in_specs=[smem, hbm],
        out_specs=vmem,
        scratch_shapes=[
            pltpu.VMEM(((reach + 1) * cap, 2, strip, side + LANES), f32),
            pltpu.SemaphoreType.DMA(((reach + 1) * cap,)),
        ],
        compiler_params=params(),
        name="cut",
    )(tables, object_field)
    pieces = [cuts[0]] + [passed_along(cuts[j], "tile", -j) for j in range(1, reach + 1)]

    factors = cosine_factors(width)
    half_tables = pl.pallas_call(
        table_kernel,
        out_shape=[shape((half, half), bf16)] * 4,
        in_specs=[vmem],
        out_specs=[vmem] * 4,
        compiler_params=params(),
        cost_estimate=pl.CostEstimate(
            flops=half * half * 10, bytes_accessed=half * half * 8, transcendentals=0
        ),
        name="tables",
    )(factors)
    local, powers, extra = decay_tables(width, strip)
    cos_part, sin_part = fourier_tables(side)

    own, away = pl.pallas_call(
        frame_kernel,
        out_shape=[
            shape((cap, 2, strip, side), f32),
            shape((reach, cap, 2, strip, side), bf16),
        ],
        in_specs=[smem, smem] + [vmem] * (5 + reach),
        out_specs=[vmem, vmem],
        scratch_shapes=[pltpu.VMEM(((reach + 1) * strip, side), f32)],
        compiler_params=params(),
        name="frames",
    )(frame_table, frame_count, probe, measured, cos_part, sin_part, *pieces)
    arrived = [passed_along(away[j - 1], "tile", j) for j in range(1, reach + 1)]

    updated = pl.pallas_call(
        place_kernel,
        out_shape=shape(object_field.shape, f32),
        in_specs=[smem, vmem, vmem] + [vmem] * reach,
        out_specs=vmem,
        compiler_params=params(),
        name="place",
    )(tables, object_field, own, *arrived)
    above = passed_along(updated[:, :, strip - 1 :], "tile", 1)
    below = passed_along(updated[:, :, :1], "tile", -1)

    solved, ends = pl.pallas_call(
        forward_kernel,
        out_shape=[shape((angles, strip, width), f32), shape((2, angles, width), f32)],
        in_specs=[vmem] * 9,
        out_specs=[vmem, vmem],
        scratch_shapes=[pltpu.VMEM((rows, width), f32)] + [pltpu.VMEM((rows, half), bf16)] * 4,
        compiler_params=params(),
        name="forward",
    )(updated, above, below, *half_tables, local, extra)
    every_end = lax.all_gather(ends, "tile")
    place = lax.axis_index("tile").astype(jnp.int32).reshape(1)
    phase_map = pl.pallas_call(
        inverse_kernel,
        out_shape=shape((angles, strip, width), f32),
        in_specs=[smem] + [vmem] * 9,
        out_specs=vmem,
        scratch_shapes=[
            pltpu.VMEM((2, angles, width), f32),
            pltpu.VMEM((rows, width), bf16),
            pltpu.VMEM((rows, width), bf16),
        ],
        compiler_params=params(),
        name="inverse",
    )(place, solved, every_end, *half_tables, local, powers, extra)
    return (updated, phase_map)


def solution(mesh):
    return jax.shard_map(
        body,
        mesh=mesh,
        in_specs=(
            P("group", None, "tile", None),
            P(),
            P(("group", "tile"), None, None),
            P(("group", "tile"), None),
            P(("group", "tile")),
        ),
        out_specs=(P("group", None, "tile", None), P("group", "tile", None)),
        check_vma=False,
    )
```

```python
import functools
import math

import numpy as np
import jax
import jax.numpy as jnp
from jax import lax
from jax.experimental import pallas as pl
from jax.experimental.pallas import tpu as pltpu
from jax.sharding import PartitionSpec as P

magnitude_floor = 0.5
soften_term = 0.5
screen_term = 0.0001
epsilon_term = 1e-06
f32 = jnp.float32
bf16 = jnp.bfloat16
LANES = 128
GROUP = 8
TILE = 256
VMEM_BYTES = 30 * 1024 * 1024
MESH = pl.DeviceIdType.MESH
vmem = pl.BlockSpec(memory_space=pltpu.VMEM)
smem = pl.BlockSpec(memory_space=pltpu.SMEM)
hbm = pl.BlockSpec(memory_space=pl.ANY)


def params(**more):
    return pltpu.CompilerParams(vmem_limit_bytes=VMEM_BYTES, **more)


def exchange_kernel(moves, keep, source, out, send_sems, recv_sems):
    count = lax.axis_size("tile")
    me = lax.axis_index("tile")
    barrier = pltpu.get_barrier_semaphore()
    met = jnp.zeros((), jnp.int32)
    for by in sorted({sign * by for _, _, by in moves for sign in (1, -1)}):
        there = (me + by >= 0) & (me + by < count)

        @pl.when(there)
        def _():
            pl.semaphore_signal(
                barrier, inc=1, device_id={"tile": me + by}, device_id_type=MESH
            )

        met = met + jnp.where(there, 1, 0)
    pl.semaphore_wait(barrier, met)
    copies = []
    for index, (first, last, by) in enumerate(moves):
        copy = pltpu.make_async_remote_copy(
            src_ref=source.at[first],
            dst_ref=out.at[last],
            send_sem=send_sems.at[index],
            recv_sem=recv_sems.at[index],
            device_id={"tile": me + by},
            device_id_type=MESH,
        )
        sends = (me + by >= 0) & (me + by < count)
        takes = (me - by >= 0) & (me - by < count)
        copies.append((copy, sends, takes, last))
        pl.when(sends)(copy.start)
    for first, last in keep:
        out[last] = source[first]
    for copy, sends, takes, last in copies:

        @pl.when(jnp.logical_not(takes))
        def _():
            out[last] = jnp.zeros(out.shape[1:], out.dtype)

    for copy, sends, takes, last in copies:
        pl.when(takes)(copy.wait_recv)
        pl.when(sends)(copy.wait_send)


def exchanged(source, slots, moves, keep, number, name):
    return pl.pallas_call(
        functools.partial(exchange_kernel, moves, keep),
        out_shape=jax.ShapeDtypeStruct((slots,) + source.shape[1:], source.dtype),
        in_specs=[vmem],
        out_specs=vmem,
        scratch_shapes=[pltpu.SemaphoreType.DMA((len(moves),))] * 2,
        compiler_params=params(collective_id=number, has_side_effects=True),
        name=name,
    )(source)


def join_kernel(ends, powers, extra, out, heard, told, up_sems, in_sems, down_sems, back_sems):
    count = lax.axis_size("tile")
    me = lax.axis_index("tile")
    blocks, lines = ends.shape[0], ends.shape[1]
    angles = lines // 2
    stride = count // blocks
    mine = me // stride
    joins = lax.rem(me, stride) == 0
    barrier = pltpu.get_barrier_semaphore()

    def greet(by, _):
        pl.semaphore_signal(
            barrier, inc=1, device_id={"tile": lax.rem(me + by, count)}, device_id_type=MESH
        )
        return 0

    lax.fori_loop(1, count, greet, 0)
    pl.semaphore_wait(barrier, count - 1)

    def up(by):
        block = lax.rem(mine + by, blocks)
        return pltpu.make_async_remote_copy(
            src_ref=ends.at[block],
            dst_ref=heard.at[me],
            send_sem=up_sems.at[block],
            recv_sem=in_sems.at[me],
            device_id={"tile": block * stride},
            device_id_type=MESH,
        )

    def came(other):
        return pltpu.make_async_remote_copy(
            src_ref=ends.at[0],
            dst_ref=heard.at[other],
            send_sem=up_sems.at[0],
            recv_sem=in_sems.at[other],
            device_id={"tile": other},
            device_id_type=MESH,
        )

    def down(other):
        return pltpu.make_async_remote_copy(
            src_ref=told.at[other],
            dst_ref=out.at[mine],
            send_sem=down_sems.at[other],
            recv_sem=back_sems.at[mine],
            device_id={"tile": other},
            device_id_type=MESH,
        )

    def answered(block):
        return pltpu.make_async_remote_copy(
            src_ref=told.at[0],
            dst_ref=out.at[block],
            send_sem=down_sems.at[0],
            recv_sem=back_sems.at[block],
            device_id={"tile": block * stride},
            device_id_type=MESH,
        )

    def each(limit, step):
        def run(index, _):
            step(index)
            return 0

        lax.fori_loop(0, limit, run, 0)

    for by in range(blocks):
        pl.when(lax.rem(mine + by, blocks) * stride != me)(lambda: up(by).start())

    @pl.when(joins)
    def _():
        heard[me] = ends[mine]
        for by in range(1, count):
            came(lax.rem(me + by, count)).wait_recv()
        step = powers[mine, 1:2]
        whole = powers[mine, count : count + 1]
        closing = extra[mine, 1:2]
        gain = extra[mine, 0:1]
        wall = heard[count - 1, angles:]
        floor = heard[0, :angles]
        for strip in range(1, count):
            floor = floor * step + heard[strip, :angles]
            wall = wall * step + heard[count - 1 - strip, angles:]
        enter = (wall + whole * floor) * closing
        leave = (floor + whole * wall) * closing
        for strip in range(count):
            told[strip, :angles] = enter * gain
            enter = enter * step + heard[strip, :angles]
            back = count - 1 - strip
            told[back, angles:] = leave * gain
            leave = leave * step + heard[back, angles:]
        for by in range(1, count):
            down(lax.rem(me + by, count)).start()
        out[mine] = told[me]

    for by in range(blocks):
        block = lax.rem(mine + by, blocks)
        pl.when(block * stride != me)(lambda: answered(block).wait_recv())
        pl.when(block * stride != me)(lambda: up(by).wait_send())

    @pl.when(joins)
    def _():
        for by in range(1, count):
            down(lax.rem(me + by, count)).wait_send()


def fourier_tables(side):
    indices = np.arange(side)
    products = indices[:, None] * indices[None, :] % side
    phases = products.astype(np.float64) * (-2.0 * math.pi / side)
    scale = 1.0 / math.sqrt(side)
    return (
        jnp.asarray(np.cos(phases) * scale, f32).astype(bf16),
        jnp.asarray(np.sin(phases) * scale, f32).astype(bf16),
    )


def cosine_factors(grid_side):
    half = grid_side // 2
    step = 32
    out = []
    for odd in (0, 1):
        freqs = 2 * np.arange(half) + odd
        scale = np.where(freqs == 0, math.sqrt(1.0 / grid_side), math.sqrt(2.0 / grid_side))
        coarse = (2 * step * np.arange(half // step)[:, None] * freqs[None, :]) % (4 * grid_side)
        fine = ((2 * np.arange(step)[:, None] + 1) * freqs[None, :]) % (4 * grid_side)
        unit = math.pi / (2 * grid_side)
        out.append(
            np.stack(
                [
                    np.cos(coarse * unit) * scale,
                    np.sin(coarse * unit) * scale,
                    np.cos(fine * unit),
                    np.sin(fine * unit),
                ]
            )
        )
    return jnp.asarray(np.stack(out), f32)


def decay_tables(grid_side, strip_rows):
    half = grid_side // 2
    freqs = np.concatenate([2 * np.arange(half), 2 * np.arange(half) + 1]).astype(np.float64)
    shift = screen_term + 2.0 - 2.0 * np.cos(freqs * math.pi / grid_side)
    rate = 2.0 * np.arcsinh(np.sqrt(shift) / 2.0)
    gain = 1.0 / (2.0 * np.sinh(rate))
    rows = np.arange(GROUP)[:, None]
    down = [np.where(rows >= s, np.exp(-s * rate), 0.0) for s in (1, 2, 4)]
    up = [np.where(rows < GROUP - s, np.exp(-s * rate), 0.0) for s in (1, 2, 4)]
    down.append(np.exp(-(rows + 1) * rate))
    up.append(np.exp(-(GROUP - rows) * rate))
    local = np.stack(down + up)
    strips = grid_side // strip_rows
    powers = np.exp(-strip_rows * np.arange(strips + 1)[:, None] * rate)
    extra = np.stack(
        [gain, 1.0 / (1.0 - np.exp(-2.0 * grid_side * rate)), np.exp(-GROUP * rate)]
        + [rate * 0.0] * 5
    )
    return local.astype(np.float32), powers.astype(np.float32), extra.astype(np.float32)


def table_kernel(factors, even_hi, even_lo, odd_hi, odd_lo):
    step = factors.shape[2]
    blocks = even_hi.shape[0] // step
    for part, (high, low) in enumerate(((even_hi, even_lo), (odd_hi, odd_lo))):
        fine_cos = factors[part, 2]
        fine_sin = factors[part, 3]
        for block in range(blocks):
            value = (
                factors[part, 0, block : block + 1] * fine_cos
                - factors[part, 1, block : block + 1] * fine_sin
            )
            rounded = value.astype(bf16)
            high[block * step : (block + 1) * step] = rounded
            low[block * step : (block + 1) * step] = (value - rounded.astype(f32)).astype(bf16)


def window_start(column, width, span):
    return jnp.minimum(column // LANES, (width - span) // LANES) * LANES


def cut_kernel(tables, field, out, buffer, sems):
    count, cap = tables.shape[0], tables.shape[1]
    width = field.shape[3]
    side = out.shape[-1]
    span = side + LANES
    jobs = [(j, s) for j in range(count) for s in range(cap)]

    def fetch(index):
        j, s = jobs[index]
        start = pl.multiple_of(window_start(tables[j, s, 1], width, span), LANES)
        return pltpu.make_async_copy(
            field.at[tables[j, s, 2], :, :, pl.ds(start, span)], buffer.at[index], sems.at[index]
        )

    for index in range(len(jobs)):
        fetch(index).start()
    for index, (j, s) in enumerate(jobs):
        fetch(index).wait()
        column = tables[j, s, 1]
        shift = column - window_start(column, width, span)
        for part in range(2):
            turned = pltpu.roll(buffer[index, part], lax.rem(span - shift, span), 1)
            out[j, s, part] = turned[:, :side].astype(bf16)


def frame_kernel(
    table, counts, probe, measured, cos_ref, sin_ref, cuts, arrived, own_out, away_out, window
):
    pieces = [cuts.at[0]] + [arrived.at[j] for j in range(arrived.shape[0])]
    cap, side = measured.shape[0], measured.shape[1]
    strip = pieces[0].shape[2]
    reach = len(pieces) - 1
    total = (reach + 1) * strip
    cos_part, sin_part = cos_ref[...], sin_ref[...]
    stacked = jnp.concatenate([cos_part, sin_part], 0)
    joined = jnp.concatenate([cos_part, sin_part], 1)
    probe_re, probe_im = probe[0], probe[1]
    peak = jnp.max(probe_re * probe_re + probe_im * probe_im) + epsilon_term

    def left(re, im, sign):
        products = jnp.dot(
            stacked, jnp.concatenate([re, im], 1), preferred_element_type=f32
        )
        cc, ci = products[:side, :side], products[:side, side:]
        sc, si = products[side:, :side], products[side:, side:]
        return (cc - si, ci + sc) if sign > 0 else (cc + si, ci - sc)

    def right(re, im, sign):
        products = jnp.dot(
            jnp.concatenate([re, im], 0), joined, preferred_element_type=f32
        )
        rc, rs = products[:side, :side], products[:side, side:]
        ic, js = products[side:, :side], products[side:, side:]
        return (rc - js, rs + ic) if sign > 0 else (rc + js, ic - rs)

    for s in range(cap):
        offset = table[s, 0]
        patch = []
        for part in range(2):
            for j in range(reach + 1):
                window[j * strip : (j + 1) * strip] = pieces[j][s, part].astype(f32)
            turned = pltpu.roll(window[...], lax.rem(total - offset, total), 0)
            patch.append(turned[:side])
        wave_re = (probe_re * patch[0] - probe_im * patch[1]).astype(bf16)
        wave_im = (probe_re * patch[1] + probe_im * patch[0]).astype(bf16)
        half_re, half_im = left(wave_re, wave_im, 1)
        spec_re, spec_im = right(half_re.astype(bf16), half_im.astype(bf16), 1)
        amplitude = jnp.sqrt(spec_re * spec_re + spec_im * spec_im)
        factor = measured[s].astype(f32) / jnp.maximum(amplitude, magnitude_floor) - 1.0
        back_re, back_im = left(
            (spec_re * factor).astype(bf16), (spec_im * factor).astype(bf16), -1
        )
        corr_re, corr_im = right(back_re.astype(bf16), back_im.astype(bf16), -1)
        live = s < counts[0]
        updates = (
            (probe_re * corr_re + probe_im * corr_im) / peak,
            (probe_re * corr_im - probe_im * corr_re) / peak,
        )
        for part in range(2):
            window[...] = jnp.zeros_like(window)
            window[:side] = jnp.where(live, updates[part], 0.0)
            turned = pltpu.roll(window[...], offset, 0)
            own_out[s, part] = turned[:strip]
            for j in range(1, reach + 1):
                away_out[j - 1, s, part] = turned[j * strip : (j + 1) * strip].astype(bf16)


def place_kernel(tables, field, own, away_ref, out, edges):
    away = [away_ref.at[j] for j in range(away_ref.shape[0])]
    width = field.shape[3]
    cap, side = own.shape[0], own.shape[3]
    span = side + LANES
    out[...] = field[...]
    pad = jnp.zeros((own.shape[2], LANES), f32)
    for j, source in enumerate((own, *away)):
        for s in range(cap):
            column = tables[j, s, 1]
            start = pl.multiple_of(window_start(column, width, span), LANES)
            shift = column - start
            angle = tables[j, s, 2]
            for part in range(2):
                value = jnp.concatenate([source[s, part].astype(f32), pad], 1)
                turned = pltpu.roll(value, shift, 1)
                out[angle, part, :, pl.ds(start, span)] = (
                    out[angle, part, :, pl.ds(start, span)] + turned
                )
    strip = field.shape[2]
    for angle in range(field.shape[0]):
        for part in range(2):
            edges[0, angle, part] = out[angle, part, :1]
            edges[1, angle, part] = out[angle, part, strip - 1 :]


def mirror(value):
    side = value.shape[1]
    rows = lax.broadcasted_iota(jnp.int32, (side, side), 0)
    columns = lax.broadcasted_iota(jnp.int32, (side, side), 1)
    swap = jnp.where(rows + columns == side - 1, 1.0, 0.0).astype(bf16)
    total = None
    for _ in range(3):
        piece = value.astype(bf16)
        value = value - piece.astype(f32)
        term = jnp.dot(piece, swap, preferred_element_type=f32)
        total = term if total is None else total + term
    return total


def split_store(value, high, low, columns):
    rounded = value.astype(bf16)
    high[:, columns] = rounded
    low[:, columns] = (value - rounded.astype(f32)).astype(bf16)


def bond(a_re, a_im, b_re, b_im):
    cross = a_re * b_im - a_im * b_re
    power = a_re * a_re + a_im * a_im + b_re * b_re + b_im * b_im + soften_term
    return 2.0 * cross / power


def forward_kernel(
    field, halo, even_hi, even_lo, odd_hi, odd_lo, local, extra,
    out, ends, source, xeh, xel, xoh, xol,
):
    angles, _, strip, width = field.shape
    half = width // 2
    block = GROUP * 2
    columns = lax.broadcasted_iota(jnp.int32, (block, width), 1)
    for angle in range(angles):
        for first in range(0, strip, block):
            here, up, down, left = [], [], [], []
            for part in range(2):
                body = field[angle, part, first : first + block]
                before = (
                    halo[0, angle, part]
                    if first == 0
                    else field[angle, part, first - 1 : first]
                )
                after = (
                    halo[1, angle, part]
                    if first + block == strip
                    else field[angle, part, first + block : first + block + 1]
                )
                here.append(body)
                up.append(jnp.concatenate([before, body[:-1]], 0))
                down.append(jnp.concatenate([body[1:], after], 0))
                left.append(jnp.where(columns == 0, 0.0, pltpu.roll(body, 1, 1)))
            row_up = bond(*up, *here)
            row_down = bond(*here, *down)
            col_left = bond(*left, *here)
            col_right = jnp.where(
                columns == width - 1, 0.0, pltpu.roll(col_left, width - 1, 1)
            )
            source[angle * strip + first : angle * strip + first + block] = -(
                row_down - row_up + col_right - col_left
            )
    for first in range(0, half, TILE):
        near = source[:, first : first + TILE]
        far = mirror(source[:, width - first - TILE : width - first])
        where = slice(first, first + TILE)
        split_store(near + far, xeh, xel, where)
        split_store(near - far, xoh, xol, where)
    for base, high, low, table_hi, table_lo in (
        (0, xeh, xel, even_hi, even_lo),
        (half, xoh, xol, odd_hi, odd_lo),
    ):
        for first in range(0, half, TILE):
            where = slice(first, first + TILE)
            source[:, base + first : base + first + TILE] = (
                jnp.dot(high[...], table_hi[:, where], preferred_element_type=f32)
                + jnp.dot(low[...], table_hi[:, where], preferred_element_type=f32)
                + jnp.dot(high[...], table_lo[:, where], preferred_element_type=f32)
            )
    groups = strip // GROUP
    for first in range(0, width, LANES):
        where = slice(first, first + LANES)
        gain = extra[0:1, where]
        for angle in range(angles):
            value = source[angle * strip : (angle + 1) * strip, where]
            value = value.reshape(groups, GROUP, LANES)
            fall, rise = value, value
            for index, by in enumerate((1, 2, 4)):
                fall = fall + local[index, :, where][None] * pltpu.roll(fall, by, 1)
                rise = rise + local[4 + index, :, where][None] * pltpu.roll(rise, GROUP - by, 1)
            falls, carry = [], None
            for group in range(groups):
                item = fall[group]
                if carry is not None:
                    item = item + local[3, :, where] * carry
                carry = item[GROUP - 1 :]
                falls.append(item)
            ends[first // LANES, angle : angle + 1] = carry
            rises, carry = [None] * groups, None
            for group in reversed(range(groups)):
                item = rise[group]
                if carry is not None:
                    item = item + local[7, :, where] * carry
                carry = item[:1]
                rises[group] = item
            ends[first // LANES, angles + angle : angles + angle + 1] = carry
            for group in range(groups):
                out[angle, group * GROUP : (group + 1) * GROUP, where] = gain * (
                    falls[group] + rises[group] - value[group]
                )


def inverse_kernel(
    value, incoming, even_hi, even_lo, odd_hi, odd_lo, local, extra, out, xh, xl
):
    angles, strip, width = value.shape
    half = width // 2
    groups = strip // GROUP
    for first in range(0, width, LANES):
        where = slice(first, first + LANES)
        for angle in range(angles):
            fall = incoming[first // LANES, angle : angle + 1]
            rise = incoming[first // LANES, angles + angle : angles + angle + 1]
            step = extra[2:3, where]
            falls, rises = [], []
            for group in range(groups):
                falls.append(fall)
                rises.append(rise)
                fall = fall * step
                rise = rise * step
            for pair in range(0, groups, 2):
                rows = []
                for group in (pair, pair + 1):
                    rows.append(
                        value[angle, group * GROUP : (group + 1) * GROUP, where]
                        + local[3, :, where] * falls[group]
                        + local[7, :, where] * rises[groups - 1 - group]
                    )
                item = jnp.concatenate(rows, 0)
                rounded = item.astype(bf16)
                start = angle * strip + pair * GROUP
                xh[start : start + 2 * GROUP, where] = rounded
                xl[start : start + 2 * GROUP, where] = (item - rounded.astype(f32)).astype(bf16)
    last = (((1,), (1,)), ((), ()))
    for first in range(0, half, TILE):
        where = slice(first, first + TILE)
        parts = []
        for base, table_hi, table_lo in ((0, even_hi, even_lo), (half, odd_hi, odd_lo)):
            high = xh[:, base : base + half]
            low = xl[:, base : base + half]
            parts.append(
                lax.dot_general(high, table_hi[where], last, preferred_element_type=f32)
                + lax.dot_general(low, table_hi[where], last, preferred_element_type=f32)
                + lax.dot_general(high, table_lo[where], last, preferred_element_type=f32)
            )
        near = parts[0] + parts[1]
        far = mirror(parts[0] - parts[1])
        for angle in range(angles):
            rows = slice(angle * strip, (angle + 1) * strip)
            out[angle, :, where] = near[rows]
            out[angle, :, width - first - TILE : width - first] = far[rows]


def body(object_field, probe, measured, frame_table, frame_count):
    angles, _, strip, width = object_field.shape
    side = probe.shape[1]
    cap = measured.shape[0]
    half = width // 2
    reach = side // strip
    rows = angles * strip
    strips = lax.axis_size("tile")
    blocks = width // LANES
    shape = jax.ShapeDtypeStruct

    tables = exchanged(
        frame_table[None], reach + 1, [(0, j, j) for j in range(1, reach + 1)], [(0, 0)], 0, "tell"
    )
    cuts = pl.pallas_call(
        cut_kernel,
        out_shape=shape((reach + 1, cap, 2, strip, side), bf16),
        in_specs=[smem, hbm],
        out_specs=vmem,
        scratch_shapes=[
            pltpu.VMEM(((reach + 1) * cap, 2, strip, side + LANES), f32),
            pltpu.SemaphoreType.DMA(((reach + 1) * cap,)),
        ],
        compiler_params=params(),
        name="cut",
    )(tables, object_field)
    arrived = exchanged(cuts, reach, [(j, j - 1, -j) for j in range(1, reach + 1)], [], 1, "fetch")

    factors = cosine_factors(width)
    half_tables = pl.pallas_call(
        table_kernel,
        out_shape=[shape((half, half), bf16)] * 4,
        in_specs=[vmem],
        out_specs=[vmem] * 4,
        compiler_params=params(),
        cost_estimate=pl.CostEstimate(
            flops=half * half * 10, bytes_accessed=half * half * 8, transcendentals=0
        ),
        name="tables",
    )(factors)
    local, powers, extra = decay_tables(width, strip)

    def by_block(table):
        return jnp.asarray(table.reshape(-1, blocks, LANES).transpose(1, 0, 2))

    cos_part, sin_part = fourier_tables(side)

    own, away = pl.pallas_call(
        frame_kernel,
        out_shape=[
            shape((cap, 2, strip, side), f32),
            shape((reach, cap, 2, strip, side), bf16),
        ],
        in_specs=[smem, smem] + [vmem] * 6,
        out_specs=[vmem, vmem],
        scratch_shapes=[pltpu.VMEM(((reach + 1) * strip, side), f32)],
        compiler_params=params(),
        name="frames",
    )(frame_table, frame_count, probe, measured, cos_part, sin_part, cuts, arrived)
    landed = exchanged(away, reach, [(j - 1, j - 1, j) for j in range(1, reach + 1)], [], 2, "give")

    updated, edges = pl.pallas_call(
        place_kernel,
        out_shape=[shape(object_field.shape, f32), shape((2, angles, 2, 1, width), f32)],
        in_specs=[smem, vmem, vmem, vmem],
        out_specs=[vmem, vmem],
        compiler_params=params(),
        name="place",
    )(tables, object_field, own, landed)
    halo = exchanged(edges, 2, [(1, 0, 1), (0, 1, -1)], [], 3, "edges")

    solved, ends = pl.pallas_call(
        forward_kernel,
        out_shape=[shape((angles, strip, width), f32), shape((blocks, 2 * angles, LANES), f32)],
        in_specs=[vmem] * 8,
        out_specs=[vmem, vmem],
        scratch_shapes=[pltpu.VMEM((rows, width), f32)] + [pltpu.VMEM((rows, half), bf16)] * 4,
        compiler_params=params(),
        name="forward",
    )(updated, halo, *half_tables, local, extra)
    incoming = pl.pallas_call(
        join_kernel,
        out_shape=shape(ends.shape, f32),
        in_specs=[vmem] * 3,
        out_specs=vmem,
        scratch_shapes=[
            pltpu.VMEM((strips, 2 * angles, LANES), f32),
            pltpu.VMEM((strips, 2 * angles, LANES), f32),
            pltpu.SemaphoreType.DMA((blocks,)),
            pltpu.SemaphoreType.DMA((strips,)),
            pltpu.SemaphoreType.DMA((strips,)),
            pltpu.SemaphoreType.DMA((blocks,)),
        ],
        compiler_params=params(collective_id=4, has_side_effects=True),
        name="join",
    )(ends, by_block(powers), by_block(extra))
    phase_map = pl.pallas_call(
        inverse_kernel,
        out_shape=shape((angles, strip, width), f32),
        in_specs=[vmem] * 8,
        out_specs=vmem,
        scratch_shapes=[
            pltpu.VMEM((rows, width), bf16),
            pltpu.VMEM((rows, width), bf16),
        ],
        compiler_params=params(),
        name="inverse",
    )(solved, incoming, *half_tables, local, extra)
    return (updated, phase_map)


def solution(mesh):
    return jax.shard_map(
        body,
        mesh=mesh,
        in_specs=(
            P("group", None, "tile", None),
            P(),
            P(("group", "tile"), None, None),
            P(("group", "tile"), None),
            P(("group", "tile")),
        ),
        out_specs=(P("group", None, "tile", None), P("group", "tile", None)),
        check_vma=False,
    )
```

```python
import functools
import math

import numpy as np
import jax
import jax.numpy as jnp
from jax import lax
from jax.experimental import pallas as pl
from jax.experimental.pallas import tpu as pltpu
from jax.sharding import PartitionSpec as P

magnitude_floor = 0.5
soften_term = 0.5
screen_term = 0.0001
epsilon_term = 1e-06
f32 = jnp.float32
bf16 = jnp.bfloat16
LANES = 128
GROUP = 8
TILE = 256
VMEM_BYTES = 30 * 1024 * 1024
MESH = pl.DeviceIdType.MESH
vmem = pl.BlockSpec(memory_space=pltpu.VMEM)
smem = pl.BlockSpec(memory_space=pltpu.SMEM)
hbm = pl.BlockSpec(memory_space=pltpu.HBM)


def cost(micros):
    return pl.CostEstimate(
        flops=0, bytes_accessed=int(micros * 3_000_000), transcendentals=0
    )


def params(**more):
    return pltpu.CompilerParams(vmem_limit_bytes=VMEM_BYTES, **more)


def exchange_kernel(moves, keep, source, out, send_sems, recv_sems):
    count = lax.axis_size("tile")
    me = lax.axis_index("tile")
    barrier = pltpu.get_barrier_semaphore()
    met = jnp.zeros((), jnp.int32)
    for by in sorted({sign * by for _, _, by in moves for sign in (1, -1)}):
        there = (me + by >= 0) & (me + by < count)

        @pl.when(there)
        def _():
            pl.semaphore_signal(
                barrier, inc=1, device_id={"tile": me + by}, device_id_type=MESH
            )

        met = met + jnp.where(there, 1, 0)
    pl.semaphore_wait(barrier, met)
    copies = []
    for index, (first, last, by) in enumerate(moves):
        copy = pltpu.make_async_remote_copy(
            src_ref=source.at[first],
            dst_ref=out.at[last],
            send_sem=send_sems.at[index],
            recv_sem=recv_sems.at[index],
            device_id={"tile": me + by},
            device_id_type=MESH,
        )
        sends = (me + by >= 0) & (me + by < count)
        takes = (me - by >= 0) & (me - by < count)
        copies.append((copy, sends, takes, last))
        pl.when(sends)(copy.start)
    for first, last in keep:
        out[last] = source[first]
    for copy, sends, takes, last in copies:

        @pl.when(jnp.logical_not(takes))
        def _():
            out[last] = jnp.zeros(out.shape[1:], out.dtype)

    for copy, sends, takes, last in copies:
        pl.when(takes)(copy.wait_recv)
        pl.when(sends)(copy.wait_send)


def exchanged(source, slots, moves, keep, number, name):
    return pl.pallas_call(
        functools.partial(exchange_kernel, moves, keep),
        out_shape=jax.ShapeDtypeStruct((slots,) + source.shape[1:], source.dtype),
        in_specs=[vmem],
        out_specs=vmem,
        scratch_shapes=[pltpu.SemaphoreType.DMA((len(moves),))] * 2,
        compiler_params=params(collective_id=number, has_side_effects=True),
        cost_estimate=cost(4),
        name=name,
    )(source)


def join_kernel(ends, powers, extra, out, heard, told, up_sems, in_sems, down_sems, back_sems):
    count = lax.axis_size("tile")
    me = lax.axis_index("tile")
    blocks, lines = ends.shape[0], ends.shape[1]
    angles = lines // 2
    stride = count // blocks
    mine = me // stride
    joins = lax.rem(me, stride) == 0
    barrier = pltpu.get_barrier_semaphore()

    def greet(by, _):
        pl.semaphore_signal(
            barrier, inc=1, device_id={"tile": lax.rem(me + by, count)}, device_id_type=MESH
        )
        return 0

    lax.fori_loop(1, count, greet, 0)
    pl.semaphore_wait(barrier, count - 1)

    def up(by):
        block = lax.rem(mine + by, blocks)
        return pltpu.make_async_remote_copy(
            src_ref=ends.at[block],
            dst_ref=heard.at[me],
            send_sem=up_sems.at[block],
            recv_sem=in_sems.at[me],
            device_id={"tile": block * stride},
            device_id_type=MESH,
        )

    def came(other):
        return pltpu.make_async_remote_copy(
            src_ref=ends.at[0],
            dst_ref=heard.at[other],
            send_sem=up_sems.at[0],
            recv_sem=in_sems.at[other],
            device_id={"tile": other},
            device_id_type=MESH,
        )

    def down(other):
        return pltpu.make_async_remote_copy(
            src_ref=told.at[other],
            dst_ref=out.at[mine],
            send_sem=down_sems.at[other],
            recv_sem=back_sems.at[mine],
            device_id={"tile": other},
            device_id_type=MESH,
        )

    def answered(block):
        return pltpu.make_async_remote_copy(
            src_ref=told.at[0],
            dst_ref=out.at[block],
            send_sem=down_sems.at[0],
            recv_sem=back_sems.at[block],
            device_id={"tile": block * stride},
            device_id_type=MESH,
        )

    def each(limit, step):
        def run(index, _):
            step(index)
            return 0

        lax.fori_loop(0, limit, run, 0)

    for by in range(blocks):
        pl.when(lax.rem(mine + by, blocks) * stride != me)(lambda: up(by).start())

    @pl.when(joins)
    def _():
        heard[me] = ends[mine]
        for by in range(1, count):
            came(lax.rem(me + by, count)).wait_recv()
        step = powers[mine, 1:2]
        whole = powers[mine, count : count + 1]
        closing = extra[mine, 1:2]
        gain = extra[mine, 0:1]
        wall = heard[count - 1, angles:]
        floor = heard[0, :angles]
        for strip in range(1, count):
            floor = floor * step + heard[strip, :angles]
            wall = wall * step + heard[count - 1 - strip, angles:]
        enter = (wall + whole * floor) * closing
        leave = (floor + whole * wall) * closing
        for strip in range(count):
            told[strip, :angles] = enter * gain
            enter = enter * step + heard[strip, :angles]
            back = count - 1 - strip
            told[back, angles:] = leave * gain
            leave = leave * step + heard[back, angles:]
        for by in range(1, count):
            down(lax.rem(me + by, count)).start()
        out[mine] = told[me]

    for by in range(blocks):
        block = lax.rem(mine + by, blocks)
        pl.when(block * stride != me)(lambda: answered(block).wait_recv())
        pl.when(block * stride != me)(lambda: up(by).wait_send())

    @pl.when(joins)
    def _():
        for by in range(1, count):
            down(lax.rem(me + by, count)).wait_send()


def fourier_tables(side):
    indices = np.arange(side)
    products = indices[:, None] * indices[None, :] % side
    phases = products.astype(np.float64) * (-2.0 * math.pi / side)
    scale = 1.0 / math.sqrt(side)
    return (
        jnp.asarray(np.cos(phases) * scale, f32).astype(bf16),
        jnp.asarray(np.sin(phases) * scale, f32).astype(bf16),
    )


def cosine_factors(grid_side):
    half = grid_side // 2
    step = 32
    out = []
    for odd in (0, 1):
        freqs = 2 * np.arange(half) + odd
        scale = np.where(freqs == 0, math.sqrt(1.0 / grid_side), math.sqrt(2.0 / grid_side))
        coarse = (2 * step * np.arange(half // step)[:, None] * freqs[None, :]) % (4 * grid_side)
        fine = ((2 * np.arange(step)[:, None] + 1) * freqs[None, :]) % (4 * grid_side)
        unit = math.pi / (2 * grid_side)
        out.append(
            np.stack(
                [
                    np.cos(coarse * unit) * scale,
                    np.sin(coarse * unit) * scale,
                    np.cos(fine * unit),
                    np.sin(fine * unit),
                ]
            )
        )
    return jnp.asarray(np.stack(out), f32)


def decay_tables(grid_side, strip_rows):
    half = grid_side // 2
    freqs = np.concatenate([2 * np.arange(half), 2 * np.arange(half) + 1]).astype(np.float64)
    shift = screen_term + 2.0 - 2.0 * np.cos(freqs * math.pi / grid_side)
    rate = 2.0 * np.arcsinh(np.sqrt(shift) / 2.0)
    gain = 1.0 / (2.0 * np.sinh(rate))
    rows = np.arange(GROUP)[:, None]
    down = [np.where(rows >= s, np.exp(-s * rate), 0.0) for s in (1, 2, 4)]
    up = [np.where(rows < GROUP - s, np.exp(-s * rate), 0.0) for s in (1, 2, 4)]
    down.append(np.exp(-(rows + 1) * rate))
    up.append(np.exp(-(GROUP - rows) * rate))
    local = np.stack(down + up)
    strips = grid_side // strip_rows
    powers = np.exp(-strip_rows * np.arange(strips + 1)[:, None] * rate)
    extra = np.stack(
        [gain, 1.0 / (1.0 - np.exp(-2.0 * grid_side * rate)), np.exp(-GROUP * rate)]
        + [rate * 0.0] * 5
    )
    return local.astype(np.float32), powers.astype(np.float32), extra.astype(np.float32)


def table_kernel(factors, even_hi, even_lo, odd_hi, odd_lo):
    step = factors.shape[2]
    blocks = even_hi.shape[0] // step
    for part, (high, low) in enumerate(((even_hi, even_lo), (odd_hi, odd_lo))):
        fine_cos = factors[part, 2]
        fine_sin = factors[part, 3]
        for block in range(blocks):
            value = (
                factors[part, 0, block : block + 1] * fine_cos
                - factors[part, 1, block : block + 1] * fine_sin
            )
            rounded = value.astype(bf16)
            high[block * step : (block + 1) * step] = rounded
            low[block * step : (block + 1) * step] = (value - rounded.astype(f32)).astype(bf16)


def window_start(column, width, span):
    return jnp.minimum(column // LANES, (width - span) // LANES) * LANES


def cut_kernel(tables, field, out, buffer, sems):
    count, cap = tables.shape[0], tables.shape[1]
    width = field.shape[3]
    side = out.shape[-1]
    span = side + LANES
    jobs = [(j, s) for j in range(count) for s in range(cap)]

    def fetch(index):
        j, s = jobs[index]
        start = pl.multiple_of(window_start(tables[j, s, 1], width, span), LANES)
        return pltpu.make_async_copy(
            field.at[tables[j, s, 2], :, :, pl.ds(start, span)], buffer.at[index], sems.at[index]
        )

    for index in range(len(jobs)):
        fetch(index).start()
    for index, (j, s) in enumerate(jobs):
        fetch(index).wait()
        column = tables[j, s, 1]
        shift = column - window_start(column, width, span)
        for part in range(2):
            turned = pltpu.roll(buffer[index, part], lax.rem(span - shift, span), 1)
            out[j, s, part] = turned[:, :side].astype(bf16)


def frame_kernel(
    table, counts, probe, measured, cos_ref, sin_ref, cuts, arrived, own_out, away_out, window
):
    pieces = [cuts.at[0]] + [arrived.at[j] for j in range(arrived.shape[0])]
    cap, side = measured.shape[0], measured.shape[1]
    strip = pieces[0].shape[2]
    reach = len(pieces) - 1
    total = (reach + 1) * strip
    cos_part, sin_part = cos_ref[...], sin_ref[...]
    stacked = jnp.concatenate([cos_part, sin_part], 0)
    joined = jnp.concatenate([cos_part, sin_part], 1)
    probe_re, probe_im = probe[0], probe[1]
    peak = jnp.max(probe_re * probe_re + probe_im * probe_im) + epsilon_term

    def left(re, im, sign):
        products = jnp.dot(
            stacked, jnp.concatenate([re, im], 1), preferred_element_type=f32
        )
        cc, ci = products[:side, :side], products[:side, side:]
        sc, si = products[side:, :side], products[side:, side:]
        return (cc - si, ci + sc) if sign > 0 else (cc + si, ci - sc)

    def right(re, im, sign):
        products = jnp.dot(
            jnp.concatenate([re, im], 0), joined, preferred_element_type=f32
        )
        rc, rs = products[:side, :side], products[:side, side:]
        ic, js = products[side:, :side], products[side:, side:]
        return (rc - js, rs + ic) if sign > 0 else (rc + js, ic - rs)

    for s in range(cap):
        offset = table[s, 0]
        patch = []
        for part in range(2):
            for j in range(reach + 1):
                window[j * strip : (j + 1) * strip] = pieces[j][s, part].astype(f32)
            turned = pltpu.roll(window[...], lax.rem(total - offset, total), 0)
            patch.append(turned[:side])
        wave_re = (probe_re * patch[0] - probe_im * patch[1]).astype(bf16)
        wave_im = (probe_re * patch[1] + probe_im * patch[0]).astype(bf16)
        half_re, half_im = left(wave_re, wave_im, 1)
        spec_re, spec_im = right(half_re.astype(bf16), half_im.astype(bf16), 1)
        amplitude = jnp.sqrt(spec_re * spec_re + spec_im * spec_im)
        factor = measured[s].astype(f32) / jnp.maximum(amplitude, magnitude_floor) - 1.0
        back_re, back_im = left(
            (spec_re * factor).astype(bf16), (spec_im * factor).astype(bf16), -1
        )
        corr_re, corr_im = right(back_re.astype(bf16), back_im.astype(bf16), -1)
        live = s < counts[0]
        updates = (
            (probe_re * corr_re + probe_im * corr_im) / peak,
            (probe_re * corr_im - probe_im * corr_re) / peak,
        )
        for part in range(2):
            window[...] = jnp.zeros_like(window)
            window[:side] = jnp.where(live, updates[part], 0.0)
            turned = pltpu.roll(window[...], offset, 0)
            own_out[s, part] = turned[:strip]
            for j in range(1, reach + 1):
                away_out[j - 1, s, part] = turned[j * strip : (j + 1) * strip].astype(bf16)


def place_kernel(tables, field, own, away_ref, updated, out, edges, sem):
    away = [away_ref.at[j] for j in range(away_ref.shape[0])]
    width = field.shape[3]
    cap, side = own.shape[0], own.shape[3]
    span = side + LANES
    out[...] = field[...]
    pad = jnp.zeros((own.shape[2], LANES), f32)
    for j, source in enumerate((own, *away)):
        for s in range(cap):
            column = tables[j, s, 1]
            start = pl.multiple_of(window_start(column, width, span), LANES)
            shift = column - start
            angle = tables[j, s, 2]
            for part in range(2):
                value = jnp.concatenate([source[s, part].astype(f32), pad], 1)
                turned = pltpu.roll(value, shift, 1)
                out[angle, part, :, pl.ds(start, span)] = (
                    out[angle, part, :, pl.ds(start, span)] + turned
                )
    strip = field.shape[2]
    for angle in range(field.shape[0]):
        for part in range(2):
            edges[0, angle, part] = out[angle, part, :1]
            edges[1, angle, part] = out[angle, part, strip - 1 :]
    copy = pltpu.make_async_copy(out, updated, sem)
    copy.start()
    copy.wait()


def mirror(value):
    side = value.shape[1]
    rows = lax.broadcasted_iota(jnp.int32, (side, side), 0)
    columns = lax.broadcasted_iota(jnp.int32, (side, side), 1)
    swap = jnp.where(rows + columns == side - 1, 1.0, 0.0).astype(bf16)
    total = None
    for _ in range(3):
        piece = value.astype(bf16)
        value = value - piece.astype(f32)
        term = jnp.dot(piece, swap, preferred_element_type=f32)
        total = term if total is None else total + term
    return total


def split_store(value, high, low, columns):
    rounded = value.astype(bf16)
    high[:, columns] = rounded
    low[:, columns] = (value - rounded.astype(f32)).astype(bf16)


def bond(a_re, a_im, b_re, b_im):
    cross = a_re * b_im - a_im * b_re
    power = a_re * a_re + a_im * a_im + b_re * b_re + b_im * b_im + soften_term
    return 2.0 * cross / power


def forward_kernel(
    field, halo, even_hi, even_lo, odd_hi, odd_lo, local, extra,
    out, ends, source, xeh, xel, xoh, xol,
):
    angles, _, strip, width = field.shape
    half = width // 2
    block = GROUP * 2
    columns = lax.broadcasted_iota(jnp.int32, (block, width), 1)
    blocks = strip // block

    def gradients(index, _):
        angle = index // blocks
        first = pl.multiple_of(lax.rem(index, blocks) * block, block)
        here, up, down, left = [], [], [], []
        for part in range(2):
            body = field[angle, part, pl.ds(first, block)]
            before = jnp.where(
                first == 0,
                halo[0, angle, part],
                field[angle, part, pl.ds(jnp.maximum(first - 1, 0), 1)],
            )
            after = jnp.where(
                first + block == strip,
                halo[1, angle, part],
                field[angle, part, pl.ds(jnp.minimum(first + block, strip - 1), 1)],
            )
            here.append(body)
            up.append(jnp.concatenate([before, body[:-1]], 0))
            down.append(jnp.concatenate([body[1:], after], 0))
            left.append(jnp.where(columns == 0, 0.0, pltpu.roll(body, 1, 1)))
        row_up = bond(*up, *here)
        row_down = bond(*here, *down)
        col_left = bond(*left, *here)
        col_right = jnp.where(columns == width - 1, 0.0, pltpu.roll(col_left, width - 1, 1))
        start = pl.multiple_of(angle * strip + first, block)
        source[pl.ds(start, block)] = -(row_down - row_up + col_right - col_left)
        return 0

    lax.fori_loop(0, angles * blocks, gradients, 0)
    for first in range(0, half, TILE):
        near = source[:, first : first + TILE]
        far = mirror(source[:, width - first - TILE : width - first])
        where = slice(first, first + TILE)
        split_store(near + far, xeh, xel, where)
        split_store(near - far, xoh, xol, where)
    for base, high, low, table_hi, table_lo in (
        (0, xeh, xel, even_hi, even_lo),
        (half, xoh, xol, odd_hi, odd_lo),
    ):
        for first in range(0, half, TILE):
            where = slice(first, first + TILE)
            source[:, base + first : base + first + TILE] = (
                jnp.dot(high[...], table_hi[:, where], preferred_element_type=f32)
                + jnp.dot(low[...], table_hi[:, where], preferred_element_type=f32)
                + jnp.dot(high[...], table_lo[:, where], preferred_element_type=f32)
            )
    groups = strip // GROUP

    def scan(chunk, _):
        where = pl.ds(pl.multiple_of(chunk * LANES, LANES), LANES)
        gain = extra[0:1, where]
        for angle in range(angles):
            value = source[angle * strip : (angle + 1) * strip, where]
            value = value.reshape(groups, GROUP, LANES)
            fall, rise = value, value
            for index, by in enumerate((1, 2, 4)):
                fall = fall + local[index, :, where][None] * pltpu.roll(fall, by, 1)
                rise = rise + local[4 + index, :, where][None] * pltpu.roll(rise, GROUP - by, 1)
            falls, carry = [], None
            for group in range(groups):
                item = fall[group]
                if carry is not None:
                    item = item + local[3, :, where] * carry
                carry = item[GROUP - 1 :]
                falls.append(item)
            ends[chunk, angle : angle + 1] = carry
            rises, carry = [None] * groups, None
            for group in reversed(range(groups)):
                item = rise[group]
                if carry is not None:
                    item = item + local[7, :, where] * carry
                carry = item[:1]
                rises[group] = item
            ends[chunk, angles + angle : angles + angle + 1] = carry
            for group in range(groups):
                out[angle, group * GROUP : (group + 1) * GROUP, where] = gain * (
                    falls[group] + rises[group] - value[group]
                )
        return 0

    lax.fori_loop(0, width // LANES, scan, 0)


def inverse_kernel(
    value, incoming, even_hi, even_lo, odd_hi, odd_lo, local, extra, out, xh, xl
):
    angles, strip, width = value.shape
    half = width // 2
    groups = strip // GROUP

    def enter(chunk, _):
        where = pl.ds(pl.multiple_of(chunk * LANES, LANES), LANES)
        for angle in range(angles):
            fall = incoming[chunk, angle : angle + 1]
            rise = incoming[chunk, angles + angle : angles + angle + 1]
            step = extra[2:3, where]
            falls, rises = [], []
            for group in range(groups):
                falls.append(fall)
                rises.append(rise)
                fall = fall * step
                rise = rise * step
            for pair in range(0, groups, 2):
                rows = []
                for group in (pair, pair + 1):
                    rows.append(
                        value[angle, group * GROUP : (group + 1) * GROUP, where]
                        + local[3, :, where] * falls[group]
                        + local[7, :, where] * rises[groups - 1 - group]
                    )
                item = jnp.concatenate(rows, 0)
                rounded = item.astype(bf16)
                start = angle * strip + pair * GROUP
                xh[start : start + 2 * GROUP, where] = rounded
                xl[start : start + 2 * GROUP, where] = (item - rounded.astype(f32)).astype(bf16)
        return 0

    lax.fori_loop(0, width // LANES, enter, 0)
    last = (((1,), (1,)), ((), ()))
    for first in range(0, half, TILE):
        where = slice(first, first + TILE)
        parts = []
        for base, table_hi, table_lo in ((0, even_hi, even_lo), (half, odd_hi, odd_lo)):
            high = xh[:, base : base + half]
            low = xl[:, base : base + half]
            parts.append(
                lax.dot_general(high, table_hi[where], last, preferred_element_type=f32)
                + lax.dot_general(low, table_hi[where], last, preferred_element_type=f32)
                + lax.dot_general(high, table_lo[where], last, preferred_element_type=f32)
            )
        near = parts[0] + parts[1]
        far = mirror(parts[0] - parts[1])
        for angle in range(angles):
            rows = slice(angle * strip, (angle + 1) * strip)
            out[angle, :, where] = near[rows]
            out[angle, :, width - first - TILE : width - first] = far[rows]


def body(object_field, probe, measured, frame_table, frame_count):
    angles, _, strip, width = object_field.shape
    side = probe.shape[1]
    cap = measured.shape[0]
    half = width // 2
    reach = side // strip
    rows = angles * strip
    strips = lax.axis_size("tile")
    blocks = width // LANES
    shape = jax.ShapeDtypeStruct

    tables = exchanged(
        frame_table[None], reach + 1, [(0, j, j) for j in range(1, reach + 1)], [(0, 0)], 0, "tell"
    )
    cuts = pl.pallas_call(
        cut_kernel,
        out_shape=shape((reach + 1, cap, 2, strip, side), bf16),
        in_specs=[smem, hbm],
        out_specs=vmem,
        scratch_shapes=[
            pltpu.VMEM(((reach + 1) * cap, 2, strip, side + LANES), f32),
            pltpu.SemaphoreType.DMA(((reach + 1) * cap,)),
        ],
        compiler_params=params(),
        cost_estimate=cost(2),
        name="cut",
    )(tables, object_field)
    arrived = exchanged(cuts, reach, [(j, j - 1, -j) for j in range(1, reach + 1)], [], 1, "fetch")

    factors = cosine_factors(width)
    half_tables = pl.pallas_call(
        table_kernel,
        out_shape=[shape((half, half), bf16)] * 4,
        in_specs=[vmem],
        out_specs=[vmem] * 4,
        compiler_params=params(),
        cost_estimate=cost(2),
        name="tables",
    )(factors)
    local, powers, extra = decay_tables(width, strip)

    def by_block(table):
        return jnp.asarray(table.reshape(-1, blocks, LANES).transpose(1, 0, 2))

    cos_part, sin_part = fourier_tables(side)

    own, away = pl.pallas_call(
        frame_kernel,
        out_shape=[
            shape((cap, 2, strip, side), f32),
            shape((reach, cap, 2, strip, side), bf16),
        ],
        in_specs=[smem, smem] + [vmem] * 6,
        out_specs=[vmem, vmem],
        scratch_shapes=[pltpu.VMEM(((reach + 1) * strip, side), f32)],
        compiler_params=params(),
        cost_estimate=cost(4),
        name="frames",
    )(frame_table, frame_count, probe, measured, cos_part, sin_part, cuts, arrived)
    landed = exchanged(away, reach, [(j - 1, j - 1, j) for j in range(1, reach + 1)], [], 2, "give")

    updated, held, edges = pl.pallas_call(
        place_kernel,
        out_shape=[shape(object_field.shape, f32)] * 2 + [shape((2, angles, 2, 1, width), f32)],
        in_specs=[smem, vmem, vmem, vmem],
        out_specs=[hbm, vmem, vmem],
        scratch_shapes=[pltpu.SemaphoreType.DMA],
        compiler_params=params(),
        cost_estimate=cost(3),
        name="place",
    )(tables, object_field, own, landed)
    halo = exchanged(edges, 2, [(1, 0, 1), (0, 1, -1)], [], 3, "edges")

    solved, ends = pl.pallas_call(
        forward_kernel,
        out_shape=[shape((angles, strip, width), f32), shape((blocks, 2 * angles, LANES), f32)],
        in_specs=[vmem] * 8,
        out_specs=[vmem, vmem],
        scratch_shapes=[pltpu.VMEM((rows, width), f32)] + [pltpu.VMEM((rows, half), bf16)] * 4,
        compiler_params=params(),
        cost_estimate=cost(9),
        name="forward",
    )(held, halo, *half_tables, local, extra)
    incoming = pl.pallas_call(
        join_kernel,
        out_shape=shape(ends.shape, f32),
        in_specs=[vmem] * 3,
        out_specs=vmem,
        scratch_shapes=[
            pltpu.VMEM((strips, 2 * angles, LANES), f32),
            pltpu.VMEM((strips, 2 * angles, LANES), f32),
            pltpu.SemaphoreType.DMA((blocks,)),
            pltpu.SemaphoreType.DMA((strips,)),
            pltpu.SemaphoreType.DMA((strips,)),
            pltpu.SemaphoreType.DMA((blocks,)),
        ],
        compiler_params=params(collective_id=4, has_side_effects=True),
        cost_estimate=cost(10),
        name="join",
    )(ends, by_block(powers), by_block(extra))
    phase_map = pl.pallas_call(
        inverse_kernel,
        out_shape=shape((angles, strip, width), f32),
        in_specs=[vmem] * 8,
        out_specs=vmem,
        scratch_shapes=[
            pltpu.VMEM((rows, width), bf16),
            pltpu.VMEM((rows, width), bf16),
        ],
        compiler_params=params(),
        cost_estimate=cost(6),
        name="inverse",
    )(solved, incoming, *half_tables, local, extra)
    return (updated, phase_map)


def solution(mesh):
    return jax.shard_map(
        body,
        mesh=mesh,
        in_specs=(
            P("group", None, "tile", None),
            P(),
            P(("group", "tile"), None, None),
            P(("group", "tile"), None),
            P(("group", "tile")),
        ),
        out_specs=(P("group", None, "tile", None), P("group", "tile", None)),
        check_vma=False,
    )
```

```python
import functools
import math

import numpy as np
import jax
import jax.numpy as jnp
from jax import lax
from jax.experimental import pallas as pl
from jax.experimental.pallas import tpu as pltpu
from jax.sharding import PartitionSpec as P

magnitude_floor = 0.5
soften_term = 0.5
screen_term = 0.0001
epsilon_term = 1e-06
f32 = jnp.float32
bf16 = jnp.bfloat16
LANES = 128
GROUP = 8
TILE = 256
VMEM_BYTES = 30 * 1024 * 1024
MESH = pl.DeviceIdType.MESH
vmem = pl.BlockSpec(memory_space=pltpu.VMEM)
smem = pl.BlockSpec(memory_space=pltpu.SMEM)
hbm = pl.BlockSpec(memory_space=pltpu.HBM)


def cost(micros):
    return pl.CostEstimate(
        flops=0, bytes_accessed=int(micros * 3_000_000), transcendentals=0
    )


def params(**more):
    return pltpu.CompilerParams(vmem_limit_bytes=VMEM_BYTES, **more)


def exchange_kernel(moves, keep, *refs):
    arrays = (len(refs) - 2) // 2
    sources, outs = refs[:arrays], refs[arrays : 2 * arrays]
    send_sems, recv_sems = refs[2 * arrays :]
    count = lax.axis_size("tile")
    me = lax.axis_index("tile")
    barrier = pltpu.get_barrier_semaphore()
    met = jnp.zeros((), jnp.int32)
    for by in sorted({sign * by for *_, by in moves for sign in (1, -1)}):
        there = (me + by >= 0) & (me + by < count)

        @pl.when(there)
        def _():
            pl.semaphore_signal(
                barrier, inc=1, device_id={"tile": me + by}, device_id_type=MESH
            )

        met = met + jnp.where(there, 1, 0)
    pl.semaphore_wait(barrier, met)
    copies = []
    for index, (array, first, last, by) in enumerate(moves):
        copy = pltpu.make_async_remote_copy(
            src_ref=sources[array].at[first],
            dst_ref=outs[array].at[last],
            send_sem=send_sems.at[index],
            recv_sem=recv_sems.at[index],
            device_id={"tile": me + by},
            device_id_type=MESH,
        )
        sends = (me + by >= 0) & (me + by < count)
        takes = (me - by >= 0) & (me - by < count)
        copies.append((copy, sends, takes, outs[array], last))
        pl.when(sends)(copy.start)
    for array, first, last in keep:
        outs[array][last] = sources[array][first]
    for copy, sends, takes, out, last in copies:

        @pl.when(jnp.logical_not(takes))
        def _():
            out[last] = jnp.zeros(out.shape[1:], out.dtype)

    for copy, sends, takes, out, last in copies:
        pl.when(takes)(copy.wait_recv)
        pl.when(sends)(copy.wait_send)


def exchanged(sources, slots, moves, keep, number, name):
    return pl.pallas_call(
        functools.partial(exchange_kernel, moves, keep),
        out_shape=[
            jax.ShapeDtypeStruct((slot,) + source.shape[1:], source.dtype)
            for slot, source in zip(slots, sources)
        ],
        in_specs=[vmem] * len(sources),
        out_specs=[vmem] * len(sources),
        scratch_shapes=[pltpu.SemaphoreType.DMA((len(moves),))] * 2,
        compiler_params=params(collective_id=number, has_side_effects=True),
        cost_estimate=cost(4),
        name=name,
    )(*sources)


def join_kernel(ends, powers, extra, out, heard, told, up_sems, in_sems, down_sems, back_sems):
    count = lax.axis_size("tile")
    me = lax.axis_index("tile")
    blocks, lines = ends.shape[0], ends.shape[1]
    angles = lines // 2
    stride = count // blocks
    mine = me // stride
    joins = lax.rem(me, stride) == 0
    barrier = pltpu.get_barrier_semaphore()

    def greet(by, _):
        pl.semaphore_signal(
            barrier, inc=1, device_id={"tile": lax.rem(me + by, count)}, device_id_type=MESH
        )
        return 0

    lax.fori_loop(1, count, greet, 0)
    pl.semaphore_wait(barrier, count - 1)

    def up(by):
        block = lax.rem(mine + by, blocks)
        return pltpu.make_async_remote_copy(
            src_ref=ends.at[block],
            dst_ref=heard.at[me],
            send_sem=up_sems.at[block],
            recv_sem=in_sems.at[me],
            device_id={"tile": block * stride},
            device_id_type=MESH,
        )

    def came(other):
        return pltpu.make_async_remote_copy(
            src_ref=ends.at[0],
            dst_ref=heard.at[other],
            send_sem=up_sems.at[0],
            recv_sem=in_sems.at[other],
            device_id={"tile": other},
            device_id_type=MESH,
        )

    def down(other):
        return pltpu.make_async_remote_copy(
            src_ref=told.at[other],
            dst_ref=out.at[mine],
            send_sem=down_sems.at[other],
            recv_sem=back_sems.at[mine],
            device_id={"tile": other},
            device_id_type=MESH,
        )

    def answered(block):
        return pltpu.make_async_remote_copy(
            src_ref=told.at[0],
            dst_ref=out.at[block],
            send_sem=down_sems.at[0],
            recv_sem=back_sems.at[block],
            device_id={"tile": block * stride},
            device_id_type=MESH,
        )

    def each(limit, step):
        def run(index, _):
            step(index)
            return 0

        lax.fori_loop(0, limit, run, 0)

    for by in range(blocks):
        pl.when(lax.rem(mine + by, blocks) * stride != me)(lambda: up(by).start())

    @pl.when(joins)
    def _():
        heard[me] = ends[mine]
        for by in range(1, count):
            came(lax.rem(me + by, count)).wait_recv()
        step = powers[mine, 1:2]
        whole = powers[mine, count : count + 1]
        closing = extra[mine, 1:2]
        gain = extra[mine, 0:1]
        wall = heard[count - 1, angles:]
        floor = heard[0, :angles]
        for strip in range(1, count):
            floor = floor * step + heard[strip, :angles]
            wall = wall * step + heard[count - 1 - strip, angles:]
        enter = (wall + whole * floor) * closing
        leave = (floor + whole * wall) * closing
        for strip in range(count):
            told[strip, :angles] = enter * gain
            enter = enter * step + heard[strip, :angles]
            back = count - 1 - strip
            told[back, angles:] = leave * gain
            leave = leave * step + heard[back, angles:]
        for by in range(1, count):
            down(lax.rem(me + by, count)).start()
        out[mine] = told[me]

    for by in range(blocks):
        block = lax.rem(mine + by, blocks)
        pl.when(block * stride != me)(lambda: answered(block).wait_recv())
        pl.when(block * stride != me)(lambda: up(by).wait_send())

    @pl.when(joins)
    def _():
        for by in range(1, count):
            down(lax.rem(me + by, count)).wait_send()


def fourier_tables(side):
    indices = np.arange(side)
    products = indices[:, None] * indices[None, :] % side
    phases = products.astype(np.float64) * (-2.0 * math.pi / side)
    scale = 1.0 / math.sqrt(side)
    return (
        jnp.asarray(np.cos(phases) * scale, f32).astype(bf16),
        jnp.asarray(np.sin(phases) * scale, f32).astype(bf16),
    )


def cosine_factors(grid_side):
    half = grid_side // 2
    step = 32
    out = []
    for odd in (0, 1):
        freqs = 2 * np.arange(half) + odd
        scale = np.where(freqs == 0, math.sqrt(1.0 / grid_side), math.sqrt(2.0 / grid_side))
        coarse = (2 * step * np.arange(half // step)[:, None] * freqs[None, :]) % (4 * grid_side)
        fine = ((2 * np.arange(step)[:, None] + 1) * freqs[None, :]) % (4 * grid_side)
        unit = math.pi / (2 * grid_side)
        out.append(
            np.stack(
                [
                    np.cos(coarse * unit) * scale,
                    np.sin(coarse * unit) * scale,
                    np.cos(fine * unit),
                    np.sin(fine * unit),
                ]
            )
        )
    return jnp.asarray(np.stack(out), f32)


def decay_tables(grid_side, strip_rows):
    half = grid_side // 2
    freqs = np.concatenate([2 * np.arange(half), 2 * np.arange(half) + 1]).astype(np.float64)
    shift = screen_term + 2.0 - 2.0 * np.cos(freqs * math.pi / grid_side)
    rate = 2.0 * np.arcsinh(np.sqrt(shift) / 2.0)
    gain = 1.0 / (2.0 * np.sinh(rate))
    rows = np.arange(GROUP)[:, None]
    down = [np.where(rows >= s, np.exp(-s * rate), 0.0) for s in (1, 2, 4)]
    up = [np.where(rows < GROUP - s, np.exp(-s * rate), 0.0) for s in (1, 2, 4)]
    down.append(np.exp(-(rows + 1) * rate))
    up.append(np.exp(-(GROUP - rows) * rate))
    local = np.stack(down + up)
    strips = grid_side // strip_rows
    powers = np.exp(-strip_rows * np.arange(strips + 1)[:, None] * rate)
    extra = np.stack(
        [gain, 1.0 / (1.0 - np.exp(-2.0 * grid_side * rate)), np.exp(-GROUP * rate)]
        + [rate * 0.0] * 5
    )
    return local.astype(np.float32), powers.astype(np.float32), extra.astype(np.float32)


def table_kernel(factors, even_hi, even_lo, odd_hi, odd_lo):
    step = factors.shape[2]
    blocks = even_hi.shape[0] // step
    for part, (high, low) in enumerate(((even_hi, even_lo), (odd_hi, odd_lo))):
        fine_cos = factors[part, 2]
        fine_sin = factors[part, 3]
        for block in range(blocks):
            value = (
                factors[part, 0, block : block + 1] * fine_cos
                - factors[part, 1, block : block + 1] * fine_sin
            )
            rounded = value.astype(bf16)
            high[block * step : (block + 1) * step] = rounded
            low[block * step : (block + 1) * step] = (value - rounded.astype(f32)).astype(bf16)


def window_start(column, width, span):
    return jnp.minimum(column // LANES, (width - span) // LANES) * LANES


def cut_kernel(tables, field, out, buffer, sems):
    count, cap = out.shape[0], out.shape[1]
    width = field.shape[3]
    side = out.shape[-1]
    span = side + LANES
    jobs = [(j, s) for j in range(count) for s in range(cap)]

    def fetch(index):
        j, s = jobs[index]
        start = pl.multiple_of(window_start(tables[j, s, 1], width, span), LANES)
        return pltpu.make_async_copy(
            field.at[tables[j, s, 2], :, :, pl.ds(start, span)], buffer.at[index], sems.at[index]
        )

    for index in range(len(jobs)):
        fetch(index).start()
    for index, (j, s) in enumerate(jobs):
        fetch(index).wait()
        column = tables[j, s, 1]
        shift = column - window_start(column, width, span)
        for part in range(2):
            turned = pltpu.roll(buffer[index, part], lax.rem(span - shift, span), 1)
            out[j, s, part] = turned[:, :side].astype(bf16)


def frame_kernel(
    tables, probe, moved, cos_ref, sin_ref, arrived, own_out, away_out, window
):
    pieces = [arrived.at[j] for j in range(arrived.shape[0])]
    measured = moved.at[0]
    cap, side = measured.shape[0], measured.shape[1]
    strip = pieces[0].shape[2]
    reach = len(pieces) - 1
    middle = reach // 2
    total = (reach + 1) * strip
    cos_part, sin_part = cos_ref[...], sin_ref[...]
    stacked = jnp.concatenate([cos_part, sin_part], 0)
    joined = jnp.concatenate([cos_part, sin_part], 1)
    probe_re, probe_im = probe[0], probe[1]
    peak = jnp.max(probe_re * probe_re + probe_im * probe_im) + epsilon_term

    def left(re, im, sign):
        products = jnp.dot(
            stacked, jnp.concatenate([re, im], 1), preferred_element_type=f32
        )
        cc, ci = products[:side, :side], products[:side, side:]
        sc, si = products[side:, :side], products[side:, side:]
        return (cc - si, ci + sc) if sign > 0 else (cc + si, ci - sc)

    def right(re, im, sign):
        products = jnp.dot(
            jnp.concatenate([re, im], 0), joined, preferred_element_type=f32
        )
        rc, rs = products[:side, :side], products[:side, side:]
        ic, js = products[side:, :side], products[side:, side:]
        return (rc - js, rs + ic) if sign > 0 else (rc + js, ic - rs)

    for s in range(cap):
        offset = tables[middle, s, 0]
        patch = []
        for part in range(2):
            for j in range(reach + 1):
                window[j * strip : (j + 1) * strip] = pieces[j][s, part].astype(f32)
            turned = pltpu.roll(window[...], lax.rem(total - offset, total), 0)
            patch.append(turned[:side])
        wave_re = (probe_re * patch[0] - probe_im * patch[1]).astype(bf16)
        wave_im = (probe_re * patch[1] + probe_im * patch[0]).astype(bf16)
        half_re, half_im = left(wave_re, wave_im, 1)
        spec_re, spec_im = right(half_re.astype(bf16), half_im.astype(bf16), 1)
        amplitude = jnp.sqrt(spec_re * spec_re + spec_im * spec_im)
        factor = measured[s].astype(f32) / jnp.maximum(amplitude, magnitude_floor) - 1.0
        back_re, back_im = left(
            (spec_re * factor).astype(bf16), (spec_im * factor).astype(bf16), -1
        )
        corr_re, corr_im = right(back_re.astype(bf16), back_im.astype(bf16), -1)
        live = s < tables[middle, cap, 0]
        updates = (
            (probe_re * corr_re + probe_im * corr_im) / peak,
            (probe_re * corr_im - probe_im * corr_re) / peak,
        )
        for part in range(2):
            window[...] = jnp.zeros_like(window)
            window[:side] = jnp.where(live, updates[part], 0.0)
            turned = pltpu.roll(window[...], offset, 0)
            for j in range(reach + 1):
                piece = turned[j * strip : (j + 1) * strip]
                if j == middle:
                    own_out[s, part] = piece
                else:
                    away_out[j, s, part] = piece.astype(bf16)


def place_kernel(tables, field, own, away_ref, updated, out, edges, sem):
    pieces = [away_ref.at[j] for j in range(away_ref.shape[0])]
    pieces[(len(pieces) - 1) // 2] = own
    width = field.shape[3]
    cap, side = own.shape[0], own.shape[3]
    span = side + LANES
    out[...] = field[...]
    pad = jnp.zeros((own.shape[2], LANES), f32)
    for j, source in enumerate(pieces):
        for s in range(cap):
            column = tables[j, s, 1]
            start = pl.multiple_of(window_start(column, width, span), LANES)
            shift = column - start
            angle = tables[j, s, 2]
            for part in range(2):
                value = jnp.concatenate([source[s, part].astype(f32), pad], 1)
                turned = pltpu.roll(value, shift, 1)
                out[angle, part, :, pl.ds(start, span)] = (
                    out[angle, part, :, pl.ds(start, span)] + turned
                )
    strip = field.shape[2]
    for angle in range(field.shape[0]):
        for part in range(2):
            edges[0, angle, part] = out[angle, part, :1]
            edges[1, angle, part] = out[angle, part, strip - 1 :]
    copy = pltpu.make_async_copy(out, updated, sem)
    copy.start()
    copy.wait()


def mirror(value):
    side = value.shape[1]
    rows = lax.broadcasted_iota(jnp.int32, (side, side), 0)
    columns = lax.broadcasted_iota(jnp.int32, (side, side), 1)
    swap = jnp.where(rows + columns == side - 1, 1.0, 0.0).astype(bf16)
    total = None
    for _ in range(3):
        piece = value.astype(bf16)
        value = value - piece.astype(f32)
        term = jnp.dot(piece, swap, preferred_element_type=f32)
        total = term if total is None else total + term
    return total


def split_store(value, high, low, columns):
    rounded = value.astype(bf16)
    high[:, columns] = rounded
    low[:, columns] = (value - rounded.astype(f32)).astype(bf16)


def bond(a_re, a_im, b_re, b_im):
    cross = a_re * b_im - a_im * b_re
    power = a_re * a_re + a_im * a_im + b_re * b_re + b_im * b_im + soften_term
    return 2.0 * cross / power


def forward_kernel(
    field, halo, even_hi, even_lo, odd_hi, odd_lo, local, extra,
    out, ends, source, xeh, xel, xoh, xol,
):
    angles, _, strip, width = field.shape
    half = width // 2
    block = GROUP * 2
    columns = lax.broadcasted_iota(jnp.int32, (block, width), 1)
    for angle in range(angles):
        for first in range(0, strip, block):
            here, up, down, left = [], [], [], []
            for part in range(2):
                body = field[angle, part, first : first + block]
                before = (
                    halo[0, angle, part]
                    if first == 0
                    else field[angle, part, first - 1 : first]
                )
                after = (
                    halo[1, angle, part]
                    if first + block == strip
                    else field[angle, part, first + block : first + block + 1]
                )
                here.append(body)
                up.append(jnp.concatenate([before, body[:-1]], 0))
                down.append(jnp.concatenate([body[1:], after], 0))
                left.append(jnp.where(columns == 0, 0.0, pltpu.roll(body, 1, 1)))
            row_up = bond(*up, *here)
            row_down = bond(*here, *down)
            col_left = bond(*left, *here)
            col_right = jnp.where(
                columns == width - 1, 0.0, pltpu.roll(col_left, width - 1, 1)
            )
            source[angle * strip + first : angle * strip + first + block] = -(
                row_down - row_up + col_right - col_left
            )
    for first in range(0, half, TILE):
        near = source[:, first : first + TILE]
        far = mirror(source[:, width - first - TILE : width - first])
        where = slice(first, first + TILE)
        split_store(near + far, xeh, xel, where)
        split_store(near - far, xoh, xol, where)
    for base, high, low, table_hi, table_lo in (
        (0, xeh, xel, even_hi, even_lo),
        (half, xoh, xol, odd_hi, odd_lo),
    ):
        for first in range(0, half, TILE):
            where = slice(first, first + TILE)
            source[:, base + first : base + first + TILE] = (
                jnp.dot(high[...], table_hi[:, where], preferred_element_type=f32)
                + jnp.dot(low[...], table_hi[:, where], preferred_element_type=f32)
                + jnp.dot(high[...], table_lo[:, where], preferred_element_type=f32)
            )
    groups = strip // GROUP

    def scan(chunk, _):
        where = pl.ds(pl.multiple_of(chunk * LANES, LANES), LANES)
        gain = extra[0:1, where]
        for angle in range(angles):
            value = source[angle * strip : (angle + 1) * strip, where]
            value = value.reshape(groups, GROUP, LANES)
            fall, rise = value, value
            for index, by in enumerate((1, 2, 4)):
                fall = fall + local[index, :, where][None] * pltpu.roll(fall, by, 1)
                rise = rise + local[4 + index, :, where][None] * pltpu.roll(rise, GROUP - by, 1)
            falls, carry = [], None
            for group in range(groups):
                item = fall[group]
                if carry is not None:
                    item = item + local[3, :, where] * carry
                carry = item[GROUP - 1 :]
                falls.append(item)
            ends[chunk, angle : angle + 1] = carry
            rises, carry = [None] * groups, None
            for group in reversed(range(groups)):
                item = rise[group]
                if carry is not None:
                    item = item + local[7, :, where] * carry
                carry = item[:1]
                rises[group] = item
            ends[chunk, angles + angle : angles + angle + 1] = carry
            for group in range(groups):
                out[angle, group * GROUP : (group + 1) * GROUP, where] = gain * (
                    falls[group] + rises[group] - value[group]
                )
        return 0

    lax.fori_loop(0, width // LANES, scan, 0)


def inverse_kernel(
    value, incoming, even_hi, even_lo, odd_hi, odd_lo, local, extra, out, xh, xl
):
    angles, strip, width = value.shape
    half = width // 2
    groups = strip // GROUP

    def enter(chunk, _):
        where = pl.ds(pl.multiple_of(chunk * LANES, LANES), LANES)
        for angle in range(angles):
            fall = incoming[chunk, angle : angle + 1]
            rise = incoming[chunk, angles + angle : angles + angle + 1]
            step = extra[2:3, where]
            falls, rises = [], []
            for group in range(groups):
                falls.append(fall)
                rises.append(rise)
                fall = fall * step
                rise = rise * step
            for pair in range(0, groups, 2):
                rows = []
                for group in (pair, pair + 1):
                    rows.append(
                        value[angle, group * GROUP : (group + 1) * GROUP, where]
                        + local[3, :, where] * falls[group]
                        + local[7, :, where] * rises[groups - 1 - group]
                    )
                item = jnp.concatenate(rows, 0)
                rounded = item.astype(bf16)
                start = angle * strip + pair * GROUP
                xh[start : start + 2 * GROUP, where] = rounded
                xl[start : start + 2 * GROUP, where] = (item - rounded.astype(f32)).astype(bf16)
        return 0

    lax.fori_loop(0, width // LANES, enter, 0)
    last = (((1,), (1,)), ((), ()))
    for first in range(0, half, TILE):
        where = slice(first, first + TILE)
        parts = []
        for base, table_hi, table_lo in ((0, even_hi, even_lo), (half, odd_hi, odd_lo)):
            high = xh[:, base : base + half]
            low = xl[:, base : base + half]
            parts.append(
                lax.dot_general(high, table_hi[where], last, preferred_element_type=f32)
                + lax.dot_general(low, table_hi[where], last, preferred_element_type=f32)
                + lax.dot_general(high, table_lo[where], last, preferred_element_type=f32)
            )
        near = parts[0] + parts[1]
        far = mirror(parts[0] - parts[1])
        for angle in range(angles):
            rows = slice(angle * strip, (angle + 1) * strip)
            out[angle, :, where] = near[rows]
            out[angle, :, width - first - TILE : width - first] = far[rows]


def body(object_field, probe, measured, frame_table, frame_count):
    angles, _, strip, width = object_field.shape
    side = probe.shape[1]
    cap = measured.shape[0]
    half = width // 2
    reach = side // strip
    rows = angles * strip
    strips = lax.axis_size("tile")
    blocks = width // LANES
    shape = jax.ShapeDtypeStruct

    middle = reach // 2
    others = [j for j in range(reach + 1) if j != middle]
    record = jnp.concatenate(
        [frame_table, jnp.pad(frame_count[:, None], ((0, 0), (0, 2)))]
    )
    moves = [(0, 0, j, j) for j in range(1, reach + 1)]
    keep = [(0, 0, 0)]
    if middle:
        moves.append((1, 0, 0, middle))
    else:
        keep.append((1, 0, 0))
    tables, moved = exchanged(
        [record[None], measured[None]], [reach + 1, 1], moves, keep, 0, "tell"
    )
    cuts = pl.pallas_call(
        cut_kernel,
        out_shape=shape((reach + 1, cap, 2, strip, side), bf16),
        in_specs=[smem, hbm],
        out_specs=vmem,
        scratch_shapes=[
            pltpu.VMEM(((reach + 1) * cap, 2, strip, side + LANES), f32),
            pltpu.SemaphoreType.DMA(((reach + 1) * cap,)),
        ],
        compiler_params=params(),
        cost_estimate=cost(2),
        name="cut",
    )(tables, object_field)
    (arrived,) = exchanged(
        [cuts], [reach + 1], [(0, j, j, middle - j) for j in others], [(0, middle, middle)], 1, "fetch"
    )

    factors = cosine_factors(width)
    half_tables = pl.pallas_call(
        table_kernel,
        out_shape=[shape((half, half), bf16)] * 4,
        in_specs=[vmem],
        out_specs=[vmem] * 4,
        compiler_params=params(),
        cost_estimate=cost(2),
        name="tables",
    )(factors)
    local, powers, extra = decay_tables(width, strip)

    def by_block(table):
        return jnp.asarray(table.reshape(-1, blocks, LANES).transpose(1, 0, 2))

    cos_part, sin_part = fourier_tables(side)

    own, away = pl.pallas_call(
        frame_kernel,
        out_shape=[
            shape((cap, 2, strip, side), f32),
            shape((reach + 1, cap, 2, strip, side), bf16),
        ],
        in_specs=[smem] + [vmem] * 5,
        out_specs=[vmem, vmem],
        scratch_shapes=[pltpu.VMEM(((reach + 1) * strip, side), f32)],
        compiler_params=params(),
        cost_estimate=cost(4),
        name="frames",
    )(tables, probe, moved, cos_part, sin_part, arrived)
    (landed,) = exchanged(
        [away], [reach + 1], [(0, j, j, j - middle) for j in others], [], 2, "give"
    )

    updated, held, edges = pl.pallas_call(
        place_kernel,
        out_shape=[shape(object_field.shape, f32)] * 2 + [shape((2, angles, 2, 1, width), f32)],
        in_specs=[smem, vmem, vmem, vmem],
        out_specs=[hbm, vmem, vmem],
        scratch_shapes=[pltpu.SemaphoreType.DMA],
        compiler_params=params(),
        cost_estimate=cost(3),
        name="place",
    )(tables, object_field, own, landed)
    (halo,) = exchanged([edges], [2], [(0, 1, 0, 1), (0, 0, 1, -1)], [], 3, "edges")

    solved, ends = pl.pallas_call(
        forward_kernel,
        out_shape=[shape((angles, strip, width), f32), shape((blocks, 2 * angles, LANES), f32)],
        in_specs=[vmem] * 8,
        out_specs=[vmem, vmem],
        scratch_shapes=[pltpu.VMEM((rows, width), f32)] + [pltpu.VMEM((rows, half), bf16)] * 4,
        compiler_params=params(),
        cost_estimate=cost(9),
        name="forward",
    )(held, halo, *half_tables, local, extra)
    incoming = pl.pallas_call(
        join_kernel,
        out_shape=shape(ends.shape, f32),
        in_specs=[vmem] * 3,
        out_specs=vmem,
        scratch_shapes=[
            pltpu.VMEM((strips, 2 * angles, LANES), f32),
            pltpu.VMEM((strips, 2 * angles, LANES), f32),
            pltpu.SemaphoreType.DMA((blocks,)),
            pltpu.SemaphoreType.DMA((strips,)),
            pltpu.SemaphoreType.DMA((strips,)),
            pltpu.SemaphoreType.DMA((blocks,)),
        ],
        compiler_params=params(collective_id=4, has_side_effects=True),
        cost_estimate=cost(10),
        name="join",
    )(ends, by_block(powers), by_block(extra))
    phase_map = pl.pallas_call(
        inverse_kernel,
        out_shape=shape((angles, strip, width), f32),
        in_specs=[vmem] * 8,
        out_specs=vmem,
        scratch_shapes=[
            pltpu.VMEM((rows, width), bf16),
            pltpu.VMEM((rows, width), bf16),
        ],
        compiler_params=params(),
        cost_estimate=cost(6),
        name="inverse",
    )(solved, incoming, *half_tables, local, extra)
    return (updated, phase_map)


def solution(mesh):
    return jax.shard_map(
        body,
        mesh=mesh,
        in_specs=(
            P("group", None, "tile", None),
            P(),
            P(("group", "tile"), None, None),
            P(("group", "tile"), None),
            P(("group", "tile")),
        ),
        out_specs=(P("group", None, "tile", None), P("group", "tile", None)),
        check_vma=False,
    )
```

```python
import functools
import math

import numpy as np
import jax
import jax.numpy as jnp
from jax import lax
from jax.experimental import pallas as pl
from jax.experimental.pallas import tpu as pltpu
from jax.sharding import PartitionSpec as P

magnitude_floor = 0.5
soften_term = 0.5
screen_term = 0.0001
epsilon_term = 1e-06
f32 = jnp.float32
bf16 = jnp.bfloat16
LANES = 128
GROUP = 8
TILE = 256
VMEM_BYTES = 30 * 1024 * 1024
MESH = pl.DeviceIdType.MESH
vmem = pl.BlockSpec(memory_space=pltpu.VMEM)
smem = pl.BlockSpec(memory_space=pltpu.SMEM)
hbm = pl.BlockSpec(memory_space=pltpu.HBM)


def cost(micros):
    return pl.CostEstimate(
        flops=0, bytes_accessed=int(micros * 3_000_000), transcendentals=0
    )


def params(**more):
    return pltpu.CompilerParams(vmem_limit_bytes=VMEM_BYTES, **more)


def exchange_kernel(moves, keep, work, arrays, inputs, *refs):
    sources, given = refs[:arrays], refs[arrays : arrays + inputs]
    outs = refs[arrays + inputs : 2 * arrays + inputs]
    made = refs[2 * arrays + inputs : -2]
    send_sems, recv_sems = refs[-2:]
    count = lax.axis_size("tile")
    me = lax.axis_index("tile")
    barrier = pltpu.get_barrier_semaphore()
    met = jnp.zeros((), jnp.int32)
    for by in sorted({sign * by for *_, by in moves for sign in (1, -1)}):
        there = (me + by >= 0) & (me + by < count)

        @pl.when(there)
        def _():
            pl.semaphore_signal(
                barrier, inc=1, device_id={"tile": me + by}, device_id_type=MESH
            )

        met = met + jnp.where(there, 1, 0)
    pl.semaphore_wait(barrier, met)
    copies = []
    for index, (array, first, last, by) in enumerate(moves):
        copy = pltpu.make_async_remote_copy(
            src_ref=sources[array].at[first],
            dst_ref=outs[array].at[last],
            send_sem=send_sems.at[index],
            recv_sem=recv_sems.at[index],
            device_id={"tile": me + by},
            device_id_type=MESH,
        )
        sends = (me + by >= 0) & (me + by < count)
        takes = (me - by >= 0) & (me - by < count)
        copies.append((copy, sends, takes, outs[array], last))
        pl.when(sends)(copy.start)
    if work is not None:
        work(*given, *made)
    for array, first, last in keep:
        outs[array][last] = sources[array][first]
    for copy, sends, takes, out, last in copies:

        @pl.when(jnp.logical_not(takes))
        def _():
            out[last] = jnp.zeros(out.shape[1:], out.dtype)

    for copy, sends, takes, out, last in copies:
        pl.when(takes)(copy.wait_recv)
        pl.when(sends)(copy.wait_send)


def exchanged(sources, slots, moves, keep, number, name, work=None, given=(), made=()):
    return pl.pallas_call(
        functools.partial(exchange_kernel, moves, keep, work, len(sources), len(given)),
        out_shape=[
            jax.ShapeDtypeStruct((slot,) + source.shape[1:], source.dtype)
            for slot, source in zip(slots, sources)
        ]
        + list(made),
        in_specs=[vmem] * (len(sources) + len(given)),
        out_specs=[vmem] * (len(sources) + len(made)),
        scratch_shapes=[pltpu.SemaphoreType.DMA((len(moves),))] * 2,
        compiler_params=params(collective_id=number, has_side_effects=True),
        cost_estimate=cost(4),
        name=name,
    )(*sources, *given)


def join_kernel(ends, powers, extra, out, heard, told, up_sems, in_sems, down_sems, back_sems):
    count = lax.axis_size("tile")
    me = lax.axis_index("tile")
    blocks, lines = ends.shape[0], ends.shape[1]
    angles = lines // 2
    stride = count // blocks
    mine = me // stride
    joins = lax.rem(me, stride) == 0
    barrier = pltpu.get_barrier_semaphore()

    def greet(by, _):
        pl.semaphore_signal(
            barrier, inc=1, device_id={"tile": lax.rem(me + by, count)}, device_id_type=MESH
        )
        return 0

    lax.fori_loop(1, count, greet, 0)
    pl.semaphore_wait(barrier, count - 1)

    def up(by):
        block = lax.rem(mine + by, blocks)
        return pltpu.make_async_remote_copy(
            src_ref=ends.at[block],
            dst_ref=heard.at[me],
            send_sem=up_sems.at[block],
            recv_sem=in_sems.at[me],
            device_id={"tile": block * stride},
            device_id_type=MESH,
        )

    def came(other):
        return pltpu.make_async_remote_copy(
            src_ref=ends.at[0],
            dst_ref=heard.at[other],
            send_sem=up_sems.at[0],
            recv_sem=in_sems.at[other],
            device_id={"tile": other},
            device_id_type=MESH,
        )

    def down(other):
        return pltpu.make_async_remote_copy(
            src_ref=told.at[other],
            dst_ref=out.at[mine],
            send_sem=down_sems.at[other],
            recv_sem=back_sems.at[mine],
            device_id={"tile": other},
            device_id_type=MESH,
        )

    def answered(block):
        return pltpu.make_async_remote_copy(
            src_ref=told.at[0],
            dst_ref=out.at[block],
            send_sem=down_sems.at[0],
            recv_sem=back_sems.at[block],
            device_id={"tile": block * stride},
            device_id_type=MESH,
        )

    def each(limit, step):
        def run(index, _):
            step(index)
            return 0

        lax.fori_loop(0, limit, run, 0)

    for by in range(blocks):
        pl.when(lax.rem(mine + by, blocks) * stride != me)(lambda: up(by).start())

    @pl.when(joins)
    def _():
        heard[me] = ends[mine]
        for by in range(1, count):
            came(lax.rem(me + by, count)).wait_recv()
        step = powers[mine, 1:2]
        whole = powers[mine, count : count + 1]
        closing = extra[mine, 1:2]
        gain = extra[mine, 0:1]
        wall = heard[count - 1, angles:]
        floor = heard[0, :angles]
        for strip in range(1, count):
            floor = floor * step + heard[strip, :angles]
            wall = wall * step + heard[count - 1 - strip, angles:]
        enter = (wall + whole * floor) * closing
        leave = (floor + whole * wall) * closing
        for strip in range(count):
            told[strip, :angles] = enter * gain
            enter = enter * step + heard[strip, :angles]
            back = count - 1 - strip
            told[back, angles:] = leave * gain
            leave = leave * step + heard[back, angles:]
        for by in range(1, count):
            down(lax.rem(me + by, count)).start()
        out[mine] = told[me]

    for by in range(blocks):
        block = lax.rem(mine + by, blocks)
        pl.when(block * stride != me)(lambda: answered(block).wait_recv())
        pl.when(block * stride != me)(lambda: up(by).wait_send())

    @pl.when(joins)
    def _():
        for by in range(1, count):
            down(lax.rem(me + by, count)).wait_send()


def fourier_tables(side):
    indices = np.arange(side)
    products = indices[:, None] * indices[None, :] % side
    phases = products.astype(np.float64) * (-2.0 * math.pi / side)
    scale = 1.0 / math.sqrt(side)
    return (
        jnp.asarray(np.cos(phases) * scale, f32).astype(bf16),
        jnp.asarray(np.sin(phases) * scale, f32).astype(bf16),
    )


def cosine_factors(grid_side):
    half = grid_side // 2
    step = 32
    out = []
    for odd in (0, 1):
        freqs = 2 * np.arange(half) + odd
        scale = np.where(freqs == 0, math.sqrt(1.0 / grid_side), math.sqrt(2.0 / grid_side))
        coarse = (2 * step * np.arange(half // step)[:, None] * freqs[None, :]) % (4 * grid_side)
        fine = ((2 * np.arange(step)[:, None] + 1) * freqs[None, :]) % (4 * grid_side)
        unit = math.pi / (2 * grid_side)
        out.append(
            np.stack(
                [
                    np.cos(coarse * unit) * scale,
                    np.sin(coarse * unit) * scale,
                    np.cos(fine * unit),
                    np.sin(fine * unit),
                ]
            )
        )
    return jnp.asarray(np.stack(out), f32)


def decay_tables(grid_side, strip_rows):
    half = grid_side // 2
    freqs = np.concatenate([2 * np.arange(half), 2 * np.arange(half) + 1]).astype(np.float64)
    shift = screen_term + 2.0 - 2.0 * np.cos(freqs * math.pi / grid_side)
    rate = 2.0 * np.arcsinh(np.sqrt(shift) / 2.0)
    gain = 1.0 / (2.0 * np.sinh(rate))
    rows = np.arange(GROUP)[:, None]
    down = [np.where(rows >= s, np.exp(-s * rate), 0.0) for s in (1, 2, 4)]
    up = [np.where(rows < GROUP - s, np.exp(-s * rate), 0.0) for s in (1, 2, 4)]
    down.append(np.exp(-(rows + 1) * rate))
    up.append(np.exp(-(GROUP - rows) * rate))
    local = np.stack(down + up)
    strips = grid_side // strip_rows
    powers = np.exp(-strip_rows * np.arange(strips + 1)[:, None] * rate)
    extra = np.stack(
        [gain, 1.0 / (1.0 - np.exp(-2.0 * grid_side * rate)), np.exp(-GROUP * rate)]
        + [rate * 0.0] * 5
    )
    return local.astype(np.float32), powers.astype(np.float32), extra.astype(np.float32)


def table_kernel(factors, even_hi, even_lo, odd_hi, odd_lo):
    step = factors.shape[2]
    blocks = even_hi.shape[0] // step
    for part, (high, low) in enumerate(((even_hi, even_lo), (odd_hi, odd_lo))):
        fine_cos = factors[part, 2]
        fine_sin = factors[part, 3]
        for block in range(blocks):
            value = (
                factors[part, 0, block : block + 1] * fine_cos
                - factors[part, 1, block : block + 1] * fine_sin
            )
            rounded = value.astype(bf16)
            high[block * step : (block + 1) * step] = rounded
            low[block * step : (block + 1) * step] = (value - rounded.astype(f32)).astype(bf16)


def window_start(column, width, span):
    return jnp.minimum(column // LANES, (width - span) // LANES) * LANES


def cut_kernel(tables, field, out, buffer, sems):
    count, cap = out.shape[0], out.shape[1]
    width = field.shape[3]
    side = out.shape[-1]
    span = side + LANES
    jobs = [(j, s) for j in range(count) for s in range(cap)]

    def fetch(index):
        j, s = jobs[index]
        start = pl.multiple_of(window_start(tables[j, s, 1], width, span), LANES)
        return pltpu.make_async_copy(
            field.at[tables[j, s, 2], :, :, pl.ds(start, span)], buffer.at[index], sems.at[index]
        )

    for index in range(len(jobs)):
        fetch(index).start()
    for index, (j, s) in enumerate(jobs):
        fetch(index).wait()
        column = tables[j, s, 1]
        shift = column - window_start(column, width, span)
        for part in range(2):
            turned = pltpu.roll(buffer[index, part], lax.rem(span - shift, span), 1)
            out[j, s, part] = turned[:, :side].astype(bf16)


def frame_kernel(
    tables, probe, moved, cos_ref, sin_ref, arrived, own_out, away_out, window
):
    pieces = [arrived.at[j] for j in range(arrived.shape[0])]
    measured = moved.at[0]
    cap, side = measured.shape[0], measured.shape[1]
    strip = pieces[0].shape[2]
    reach = len(pieces) - 1
    middle = reach // 2
    total = (reach + 1) * strip
    cos_part, sin_part = cos_ref[...], sin_ref[...]
    stacked = jnp.concatenate([cos_part, sin_part], 0)
    joined = jnp.concatenate([cos_part, sin_part], 1)
    probe_re, probe_im = probe[0], probe[1]
    peak = jnp.max(probe_re * probe_re + probe_im * probe_im) + epsilon_term

    def left(re, im, sign):
        products = jnp.dot(
            stacked, jnp.concatenate([re, im], 1), preferred_element_type=f32
        )
        cc, ci = products[:side, :side], products[:side, side:]
        sc, si = products[side:, :side], products[side:, side:]
        return (cc - si, ci + sc) if sign > 0 else (cc + si, ci - sc)

    def right(re, im, sign):
        products = jnp.dot(
            jnp.concatenate([re, im], 0), joined, preferred_element_type=f32
        )
        rc, rs = products[:side, :side], products[:side, side:]
        ic, js = products[side:, :side], products[side:, side:]
        return (rc - js, rs + ic) if sign > 0 else (rc + js, ic - rs)

    for s in range(cap):
        offset = tables[middle, s, 0]
        patch = []
        for part in range(2):
            for j in range(reach + 1):
                window[j * strip : (j + 1) * strip] = pieces[j][s, part].astype(f32)
            turned = pltpu.roll(window[...], lax.rem(total - offset, total), 0)
            patch.append(turned[:side])
        wave_re = (probe_re * patch[0] - probe_im * patch[1]).astype(bf16)
        wave_im = (probe_re * patch[1] + probe_im * patch[0]).astype(bf16)
        half_re, half_im = left(wave_re, wave_im, 1)
        spec_re, spec_im = right(half_re.astype(bf16), half_im.astype(bf16), 1)
        amplitude = jnp.sqrt(spec_re * spec_re + spec_im * spec_im)
        factor = measured[s].astype(f32) / jnp.maximum(amplitude, magnitude_floor) - 1.0
        back_re, back_im = left(
            (spec_re * factor).astype(bf16), (spec_im * factor).astype(bf16), -1
        )
        corr_re, corr_im = right(back_re.astype(bf16), back_im.astype(bf16), -1)
        live = s < tables[middle, cap, 0]
        updates = (
            (probe_re * corr_re + probe_im * corr_im) / peak,
            (probe_re * corr_im - probe_im * corr_re) / peak,
        )
        for part in range(2):
            window[...] = jnp.zeros_like(window)
            window[:side] = jnp.where(live, updates[part], 0.0)
            turned = pltpu.roll(window[...], offset, 0)
            for j in range(reach + 1):
                piece = turned[j * strip : (j + 1) * strip]
                if j == middle:
                    own_out[s, part] = piece
                else:
                    away_out[j, s, part] = piece.astype(bf16)


def place_kernel(tables, field, own, away_ref, updated, out, edges, sem):
    pieces = [away_ref.at[j] for j in range(away_ref.shape[0])]
    pieces[(len(pieces) - 1) // 2] = own
    width = field.shape[3]
    cap, side = own.shape[0], own.shape[3]
    span = side + LANES
    out[...] = field[...]
    pad = jnp.zeros((own.shape[2], LANES), f32)
    for j, source in enumerate(pieces):
        for s in range(cap):
            column = tables[j, s, 1]
            start = pl.multiple_of(window_start(column, width, span), LANES)
            shift = column - start
            angle = tables[j, s, 2]
            for part in range(2):
                value = jnp.concatenate([source[s, part].astype(f32), pad], 1)
                turned = pltpu.roll(value, shift, 1)
                out[angle, part, :, pl.ds(start, span)] = (
                    out[angle, part, :, pl.ds(start, span)] + turned
                )
    strip = field.shape[2]
    for angle in range(field.shape[0]):
        for part in range(2):
            edges[0, angle, part] = out[angle, part, :1]
            edges[1, angle, part] = out[angle, part, strip - 1 :]
    copy = pltpu.make_async_copy(out, updated, sem)
    copy.start()
    copy.wait()


def mirror(value):
    side = value.shape[1]
    rows = lax.broadcasted_iota(jnp.int32, (side, side), 0)
    columns = lax.broadcasted_iota(jnp.int32, (side, side), 1)
    swap = jnp.where(rows + columns == side - 1, 1.0, 0.0).astype(bf16)
    total = None
    for _ in range(3):
        piece = value.astype(bf16)
        value = value - piece.astype(f32)
        term = jnp.dot(piece, swap, preferred_element_type=f32)
        total = term if total is None else total + term
    return total


def split_store(value, high, low, columns):
    rounded = value.astype(bf16)
    high[:, columns] = rounded
    low[:, columns] = (value - rounded.astype(f32)).astype(bf16)


def bond(a_re, a_im, b_re, b_im):
    cross = a_re * b_im - a_im * b_re
    power = a_re * a_re + a_im * a_im + b_re * b_re + b_im * b_im + soften_term
    return 2.0 * cross / power


def forward_kernel(
    field, halo, even_hi, even_lo, odd_hi, odd_lo, local, extra,
    out, ends, source, xeh, xel, xoh, xol,
):
    angles, _, strip, width = field.shape
    half = width // 2
    block = GROUP * 2
    columns = lax.broadcasted_iota(jnp.int32, (block, width), 1)
    for angle in range(angles):
        for first in range(0, strip, block):
            here, up, down, left = [], [], [], []
            for part in range(2):
                body = field[angle, part, first : first + block]
                before = (
                    halo[0, angle, part]
                    if first == 0
                    else field[angle, part, first - 1 : first]
                )
                after = (
                    halo[1, angle, part]
                    if first + block == strip
                    else field[angle, part, first + block : first + block + 1]
                )
                here.append(body)
                up.append(jnp.concatenate([before, body[:-1]], 0))
                down.append(jnp.concatenate([body[1:], after], 0))
                left.append(jnp.where(columns == 0, 0.0, pltpu.roll(body, 1, 1)))
            row_up = bond(*up, *here)
            row_down = bond(*here, *down)
            col_left = bond(*left, *here)
            col_right = jnp.where(
                columns == width - 1, 0.0, pltpu.roll(col_left, width - 1, 1)
            )
            source[angle * strip + first : angle * strip + first + block] = -(
                row_down - row_up + col_right - col_left
            )
    for first in range(0, half, TILE):
        near = source[:, first : first + TILE]
        far = mirror(source[:, width - first - TILE : width - first])
        where = slice(first, first + TILE)
        split_store(near + far, xeh, xel, where)
        split_store(near - far, xoh, xol, where)
    for base, high, low, table_hi, table_lo in (
        (0, xeh, xel, even_hi, even_lo),
        (half, xoh, xol, odd_hi, odd_lo),
    ):
        for first in range(0, half, TILE):
            where = slice(first, first + TILE)
            source[:, base + first : base + first + TILE] = (
                jnp.dot(high[...], table_hi[:, where], preferred_element_type=f32)
                + jnp.dot(low[...], table_hi[:, where], preferred_element_type=f32)
                + jnp.dot(high[...], table_lo[:, where], preferred_element_type=f32)
            )
    groups = strip // GROUP

    def scan(chunk, _):
        where = pl.ds(pl.multiple_of(chunk * LANES, LANES), LANES)
        gain = extra[0:1, where]
        for angle in range(angles):
            value = source[angle * strip : (angle + 1) * strip, where]
            value = value.reshape(groups, GROUP, LANES)
            fall, rise = value, value
            for index, by in enumerate((1, 2, 4)):
                fall = fall + local[index, :, where][None] * pltpu.roll(fall, by, 1)
                rise = rise + local[4 + index, :, where][None] * pltpu.roll(rise, GROUP - by, 1)
            falls, carry = [], None
            for group in range(groups):
                item = fall[group]
                if carry is not None:
                    item = item + local[3, :, where] * carry
                carry = item[GROUP - 1 :]
                falls.append(item)
            ends[chunk, angle : angle + 1] = carry
            rises, carry = [None] * groups, None
            for group in reversed(range(groups)):
                item = rise[group]
                if carry is not None:
                    item = item + local[7, :, where] * carry
                carry = item[:1]
                rises[group] = item
            ends[chunk, angles + angle : angles + angle + 1] = carry
            for group in range(groups):
                out[angle, group * GROUP : (group + 1) * GROUP, where] = gain * (
                    falls[group] + rises[group] - value[group]
                )
        return 0

    lax.fori_loop(0, width // LANES, scan, 0)


def inverse_kernel(
    value, incoming, even_hi, even_lo, odd_hi, odd_lo, local, extra, out, xh, xl
):
    angles, strip, width = value.shape
    half = width // 2
    groups = strip // GROUP

    def enter(chunk, _):
        where = pl.ds(pl.multiple_of(chunk * LANES, LANES), LANES)
        for angle in range(angles):
            fall = incoming[chunk, angle : angle + 1]
            rise = incoming[chunk, angles + angle : angles + angle + 1]
            step = extra[2:3, where]
            falls, rises = [], []
            for group in range(groups):
                falls.append(fall)
                rises.append(rise)
                fall = fall * step
                rise = rise * step
            for pair in range(0, groups, 2):
                rows = []
                for group in (pair, pair + 1):
                    rows.append(
                        value[angle, group * GROUP : (group + 1) * GROUP, where]
                        + local[3, :, where] * falls[group]
                        + local[7, :, where] * rises[groups - 1 - group]
                    )
                item = jnp.concatenate(rows, 0)
                rounded = item.astype(bf16)
                start = angle * strip + pair * GROUP
                xh[start : start + 2 * GROUP, where] = rounded
                xl[start : start + 2 * GROUP, where] = (item - rounded.astype(f32)).astype(bf16)
        return 0

    lax.fori_loop(0, width // LANES, enter, 0)
    last = (((1,), (1,)), ((), ()))
    for first in range(0, half, TILE):
        where = slice(first, first + TILE)
        parts = []
        for base, table_hi, table_lo in ((0, even_hi, even_lo), (half, odd_hi, odd_lo)):
            high = xh[:, base : base + half]
            low = xl[:, base : base + half]
            parts.append(
                lax.dot_general(high, table_hi[where], last, preferred_element_type=f32)
                + lax.dot_general(low, table_hi[where], last, preferred_element_type=f32)
                + lax.dot_general(high, table_lo[where], last, preferred_element_type=f32)
            )
        near = parts[0] + parts[1]
        far = mirror(parts[0] - parts[1])
        for angle in range(angles):
            rows = slice(angle * strip, (angle + 1) * strip)
            out[angle, :, where] = near[rows]
            out[angle, :, width - first - TILE : width - first] = far[rows]


def body(object_field, probe, measured, frame_table, frame_count):
    angles, _, strip, width = object_field.shape
    side = probe.shape[1]
    cap = measured.shape[0]
    half = width // 2
    reach = side // strip
    rows = angles * strip
    strips = lax.axis_size("tile")
    blocks = width // LANES
    shape = jax.ShapeDtypeStruct

    middle = reach // 2
    others = [j for j in range(reach + 1) if j != middle]
    record = jnp.concatenate(
        [frame_table, jnp.pad(frame_count[:, None], ((0, 0), (0, 2)))]
    )
    moves = [(0, 0, j, j) for j in range(1, reach + 1)]
    keep = [(0, 0, 0)]
    if middle:
        moves.append((1, 0, 0, middle))
    else:
        keep.append((1, 0, 0))
    tables, moved = exchanged(
        [record[None], measured[None]], [reach + 1, 1], moves, keep, 0, "tell"
    )
    cuts = pl.pallas_call(
        cut_kernel,
        out_shape=shape((reach + 1, cap, 2, strip, side), bf16),
        in_specs=[smem, hbm],
        out_specs=vmem,
        scratch_shapes=[
            pltpu.VMEM(((reach + 1) * cap, 2, strip, side + LANES), f32),
            pltpu.SemaphoreType.DMA(((reach + 1) * cap,)),
        ],
        compiler_params=pltpu.CompilerParams(vmem_limit_bytes=2 * VMEM_BYTES),
        cost_estimate=cost(2),
        name="cut",
    )(tables, object_field)
    (arrived,) = exchanged(
        [cuts], [reach + 1], [(0, j, j, middle - j) for j in others], [(0, middle, middle)], 1, "fetch"
    )

    factors = cosine_factors(width)
    local, powers, extra = decay_tables(width, strip)

    def by_block(table):
        return jnp.asarray(table.reshape(-1, blocks, LANES).transpose(1, 0, 2))

    cos_part, sin_part = fourier_tables(side)

    own, away = pl.pallas_call(
        frame_kernel,
        out_shape=[
            shape((cap, 2, strip, side), f32),
            shape((reach + 1, cap, 2, strip, side), bf16),
        ],
        in_specs=[smem] + [vmem] * 5,
        out_specs=[vmem, vmem],
        scratch_shapes=[pltpu.VMEM(((reach + 1) * strip, side), f32)],
        compiler_params=params(),
        cost_estimate=cost(4),
        name="frames",
    )(tables, probe, moved, cos_part, sin_part, arrived)
    (landed,) = exchanged(
        [away], [reach + 1], [(0, j, j, j - middle) for j in others], [], 2, "give"
    )

    updated, held, edges = pl.pallas_call(
        place_kernel,
        out_shape=[shape(object_field.shape, f32)] * 2 + [shape((2, angles, 2, 1, width), f32)],
        in_specs=[smem, vmem, vmem, vmem],
        out_specs=[hbm, vmem, vmem],
        scratch_shapes=[pltpu.SemaphoreType.DMA],
        compiler_params=params(),
        cost_estimate=cost(3),
        name="place",
    )(tables, object_field, own, landed)
    halo, *half_tables = exchanged(
        [edges], [2], [(0, 1, 0, 1), (0, 0, 1, -1)], [], 3, "edges",
        table_kernel, [factors], [shape((half, half), bf16)] * 4,
    )

    solved, ends = pl.pallas_call(
        forward_kernel,
        out_shape=[shape((angles, strip, width), f32), shape((blocks, 2 * angles, LANES), f32)],
        in_specs=[vmem] * 8,
        out_specs=[vmem, vmem],
        scratch_shapes=[pltpu.VMEM((rows, width), f32)] + [pltpu.VMEM((rows, half), bf16)] * 4,
        compiler_params=params(),
        cost_estimate=cost(9),
        name="forward",
    )(held, halo, *half_tables, local, extra)
    incoming = pl.pallas_call(
        join_kernel,
        out_shape=shape(ends.shape, f32),
        in_specs=[vmem] * 3,
        out_specs=vmem,
        scratch_shapes=[
            pltpu.VMEM((strips, 2 * angles, LANES), f32),
            pltpu.VMEM((strips, 2 * angles, LANES), f32),
            pltpu.SemaphoreType.DMA((blocks,)),
            pltpu.SemaphoreType.DMA((strips,)),
            pltpu.SemaphoreType.DMA((strips,)),
            pltpu.SemaphoreType.DMA((blocks,)),
        ],
        compiler_params=params(collective_id=4, has_side_effects=True),
        cost_estimate=cost(10),
        name="join",
    )(ends, by_block(powers), by_block(extra))
    phase_map = pl.pallas_call(
        inverse_kernel,
        out_shape=shape((angles, strip, width), f32),
        in_specs=[vmem] * 8,
        out_specs=vmem,
        scratch_shapes=[
            pltpu.VMEM((rows, width), bf16),
            pltpu.VMEM((rows, width), bf16),
        ],
        compiler_params=params(),
        cost_estimate=cost(6),
        name="inverse",
    )(solved, incoming, *half_tables, local, extra)
    return (updated, phase_map)


def solution(mesh):
    return jax.shard_map(
        body,
        mesh=mesh,
        in_specs=(
            P("group", None, "tile", None),
            P(),
            P(("group", "tile"), None, None),
            P(("group", "tile"), None),
            P(("group", "tile")),
        ),
        out_specs=(P("group", None, "tile", None), P("group", "tile", None)),
        check_vma=False,
    )
```
